256 devices in a mesh: seq: 64 (over y, z, x_lo), head: 4 (over x_hi, core).
Axes of the slice: x: 4 (x_hi: 2, x_lo: 2; x = x_hi * 2 + x_lo), y: 4, z: 8, core: 2. Of those that a mesh axis runs over, the one named last changes fastest.
Arguments:
- inputs: bfloat16 [32768, 5376], P('seq'), may hold values from -6 to 6
- queries: bfloat16 [32768, 16, 128], P('seq', 'head'), may hold values from -24 to 24
- out_grad: bfloat16 [32768, 16, 128], P('seq', 'head'), may hold values from -6 to 6
- segment_ids: int32 [32768], P('seq'), may hold values from 0 to 63, never falling along the last dimension, each value on 1 to 2048 neighbouring positions
- k_weight: bfloat16 [5376, 1024], P('seq', 'head'), may hold values from -0.078125 to 0.078125
- v_weight: bfloat16 [5376, 1024], P('seq', 'head'), may hold values from -0.078125 to 0.078125
- k_gain: float32 [128], replicated, may hold values from 0.1 to 1.9
Outputs:
- inputs_grad: bfloat16 [32768, 5376], P('seq', 'head')
- query_grad: bfloat16 [32768, 16, 128], P('seq', 'head')
- k_weight_grad: float32 [5376, 1024], P('seq', 'head')
- v_weight_grad: float32 [5376, 1024], P('seq', 'head')
The draws below stay inside these ranges and needn't reach their ends.
Inputs may be any that keep to these rules, and one draw needn't show every extreme that they name: `segment_ids`: tokens of one packed document share an id; ids never fall along the row; a document holds at most 2048 tokens.
All inputs are finite; a program needn't handle non-finite values.
Results may differ from the reference program's by a relative error of at most 0.01065.
The reference program's roundings to bfloat16 on the way count: a program that leaves them out, or rounds other values in their place, can miss the bound.
Values may be sent and summed in bfloat16 or wider, within the bound.
No kernel may reach another device: no remote copies, remote signals or barrier semaphores. Data moves between devices by JAX's collectives and lax.ppermute only.
A program may use at most 128 MiB of HBM per device.

```python
import math
import jax
import jax.numpy as jnp
import numpy as np
from jax import lax

D = 5376
HEADS = 16
KV_HEADS = 8
HD = 128
WIN = 1024
TOK_DEV = 512
TOKENS = 32768
REACH = 2
N_SEQ = 64
N_HEAD = 4


def draw_queries(key, part):
    first = jax.random.fold_in(key, 0)
    dims_shape = (TOKENS, HEADS, HD)
    values = jnp.clip(jax.random.normal(first, dims_shape, jnp.float32), -6.0, 6.0)
    return values.astype(jnp.bfloat16)


def shard_levels(own_key, extent, pieces, smallest, high):
    level = 1.0
    for position, parts in pieces:
        draws = jax.random.uniform(jax.random.fold_in(jax.random.fold_in(own_key, 6), position), (parts,), jnp.float32, smallest / len(pieces), high / len(pieces))
        level = level * jnp.repeat(jnp.exp(draws), extent[position] // parts).reshape((-1,) + (1,) * (len(extent) - 1 - position))
    return level


def profile(number_of, total, limit, lean):
    loads = [(1 << 20) // math.isqrt(standing ** lean) + 1 for standing in range(2, number_of + 1)]
    rest, counts = total - limit - (number_of - 1), [1] * (number_of - 1)
    while rest > 0:
        candidates = [i for i in range(number_of - 1) if counts[i] < limit]
        pool, remaining = sum([loads[i] for i in candidates]), rest
        for i in candidates:
            extra = min(limit - counts[i], max(1, remaining * loads[i] // pool), rest)
            counts[i] = counts[i] + extra
            rest = rest - extra
    return np.array([limit] + counts)


def ragged(key, count, total, bound, slope):
    if count == 2:
        one = jax.random.randint(key, (), max(1, total - bound), min(bound, total - 1) + 1)
        return jnp.stack([one, total - one])
    lengths = jnp.asarray(profile(count, total, bound, slope), jnp.int32)
    twos = (count - 1) // 2
    giver, receiver = lengths[1:1 + 2 * twos:2], lengths[2:2 + 2 * twos:2]
    margin = jnp.minimum(giver - 1, bound - receiver)
    shifted = jax.random.randint(jax.random.fold_in(key, 1), (twos,), 0, 1 << 20) % (margin + 1)
    lengths = lengths.at[1:1 + 2 * twos:2].set(giver - shifted).at[2:2 + 2 * twos:2].set(receiver + shifted)
    return lengths[jax.random.permutation(jax.random.fold_in(key, 2), count)]


def scatter_about(key, dims, width, reach, pieces=(), kind=jnp.bfloat16):
    array = width * jax.random.normal(key, dims, jnp.float32)
    if pieces:
        array = array * shard_levels(key, dims, pieces, -0.22, 0.18)
    return jnp.clip(array, -reach, reach).astype(kind)


def setup_inputs(seed: int = 0) -> dict:
    arg_keys = jax.random.split(jax.random.key(seed), 8)
    return {
        "inputs": scatter_about(arg_keys[0], (TOKENS, D), 1.0, 6.0, ((0, 64),)),
        "queries": draw_queries(jax.random.fold_in(arg_keys[7], 71), 0),
        "out_grad": scatter_about(arg_keys[2], (TOKENS, HEADS, HD), 1.0, 6.0, ((0, 64), (1, 4))),
        "segment_ids": jnp.searchsorted(jnp.cumsum(ragged(arg_keys[3], N_SEQ, TOKENS, 4 * TOK_DEV, 2)), jnp.arange(TOKENS), side="right").astype(jnp.int32),
        "k_weight": scatter_about(arg_keys[4], (D, KV_HEADS * HD), D ** -0.5, 0.078125, ((0, 64), (1, 4))),
        "v_weight": scatter_about(arg_keys[5], (D, KV_HEADS * HD), D ** -0.5, 0.078125, ((0, 64), (1, 4))),
        "k_gain": jnp.clip(1.0 + 0.18 * jax.random.normal(arg_keys[6], (HD,), jnp.float32), 0.1, 1.9),
    }


score_scale = 168.0 ** (-0.5)

def to_low(value):
    return lax.optimization_barrier(value.astype(jnp.bfloat16)).astype(jnp.float32)

def reference(inputs, queries, out_grad, segment_ids, k_weight, v_weight, k_gain):
    group_size = HEADS // KV_HEADS
    tok_rows = TOK_DEV
    pad_rows = REACH * TOK_DEV
    span_rows = (REACH + 1) * TOK_DEV
    k_raw = jnp.dot(inputs, k_weight, preferred_element_type=jnp.float32).reshape(TOKENS, KV_HEADS, HD)
    k_inv = lax.rsqrt(lax.optimization_barrier(jnp.mean(k_raw * k_raw, axis=-1, keepdims=True)) + 1e-06)
    k_normed = k_raw * k_inv
    key_rows = (k_normed * k_gain.astype(jnp.float32)).astype(jnp.bfloat16)
    value_rows = jnp.dot(inputs, v_weight, preferred_element_type=jnp.float32).astype(jnp.bfloat16).reshape(TOKENS, KV_HEADS, HD)
    keys_pad = jnp.concatenate([jnp.zeros((pad_rows, KV_HEADS, HD), jnp.bfloat16), key_rows], 0)
    values_pad = jnp.concatenate([jnp.zeros((pad_rows, KV_HEADS, HD), jnp.bfloat16), value_rows], 0)
    seg_pad = jnp.concatenate([jnp.full((pad_rows,), -1, jnp.int32), segment_ids.astype(jnp.int32)], 0)
    query_view = queries.reshape(TOKENS, KV_HEADS, group_size, HD)
    grad_view = out_grad.reshape(TOKENS, KV_HEADS, group_size, HD)

    def visit(running, block_index):
        key_acc, value_acc = running
        first_row = (block_index * tok_rows).astype(jnp.int32)
        query_f = lax.dynamic_slice_in_dim(query_view, first_row, tok_rows, 0).astype(jnp.float32)
        grad_f = lax.dynamic_slice_in_dim(grad_view, first_row, tok_rows, 0).astype(jnp.float32)
        key_f = lax.dynamic_slice_in_dim(keys_pad, first_row, span_rows, 0).astype(jnp.float32)
        value_f = lax.dynamic_slice_in_dim(values_pad, first_row, span_rows, 0).astype(jnp.float32)
        query_seg = lax.dynamic_slice_in_dim(segment_ids.astype(jnp.int32), first_row, tok_rows, 0)
        key_seg = lax.dynamic_slice_in_dim(seg_pad, first_row, span_rows, 0)
        query_pos = first_row + jnp.arange(tok_rows, dtype=jnp.int32)
        key_pos = first_row - pad_rows + jnp.arange(span_rows, dtype=jnp.int32)
        distance = query_pos[:, None] - key_pos[None, :]
        allowed = (distance >= 0) & (distance < WIN) & (query_seg[:, None] == key_seg[None, :]) & (key_pos[None, :] >= 0)
        scores = jnp.einsum('qkgd,ckd->kgqc', query_f, key_f) * score_scale
        scores = jnp.where(allowed[None, None], scores, -1e+30)
        row_peak = lax.optimization_barrier(jnp.max(scores, axis=-1, keepdims=True))
        log_total = row_peak[..., 0] + jnp.log(lax.optimization_barrier(jnp.sum(jnp.exp(scores - row_peak), axis=-1)))
        probs = jnp.exp(scores - log_total[..., None])
        probs_low = to_low(probs)
        attn_out = jnp.einsum('kgqc,ckd->qkgd', probs_low, value_f)
        delta = jnp.transpose(lax.optimization_barrier(jnp.sum(grad_f * attn_out, axis=-1)), (1, 2, 0))
        prob_grad = jnp.einsum('qkgd,ckd->kgqc', grad_f, value_f)
        score_grad = to_low(probs * (prob_grad - delta[..., None]))
        query_grad = jnp.einsum('kgqc,ckd->qkgd', score_grad, key_f) * score_scale
        key_grad = jnp.einsum('kgqc,qkgd->ckd', score_grad, query_f) * score_scale
        value_grad = jnp.einsum('kgqc,qkgd->ckd', probs_low, grad_f)
        key_acc = lax.dynamic_update_slice_in_dim(key_acc, lax.dynamic_slice_in_dim(key_acc, first_row, span_rows, 0) + key_grad, first_row, 0)
        value_acc = lax.dynamic_update_slice_in_dim(value_acc, lax.dynamic_slice_in_dim(value_acc, first_row, span_rows, 0) + value_grad, first_row, 0)
        return ((key_acc, value_acc), query_grad.astype(jnp.bfloat16))
    empty_acc = jnp.zeros((TOKENS + pad_rows, KV_HEADS, HD), jnp.float32)
    (key_acc, value_acc), query_blocks = lax.scan(visit, (empty_acc, empty_acc), jnp.arange(N_SEQ, dtype=jnp.int32))
    query_grad = query_blocks.reshape(TOKENS, HEADS, HD)
    key_grad = key_acc[pad_rows:]
    value_grad = value_acc[pad_rows:]
    normed_grad = key_grad * k_gain.astype(jnp.float32)
    raw_grad = (normed_grad - k_normed * lax.optimization_barrier(jnp.mean(normed_grad * k_normed, axis=-1, keepdims=True))) * k_inv
    raw_low = raw_grad.astype(jnp.bfloat16).reshape(TOKENS, KV_HEADS * HD)
    value_low = value_grad.astype(jnp.bfloat16).reshape(TOKENS, KV_HEADS * HD)
    width_group = KV_HEADS // N_HEAD * HD
    inputs_total = jnp.zeros((TOKENS, D), jnp.float32)
    for group_index in range(N_HEAD):
        lower = group_index * width_group
        upper = lower + width_group
        partial_term = jnp.dot(raw_low[:, lower:upper], k_weight[:, lower:upper].T, preferred_element_type=jnp.float32)
        partial_term = partial_term + jnp.dot(value_low[:, lower:upper], v_weight[:, lower:upper].T, preferred_element_type=jnp.float32)
        inputs_total = inputs_total + partial_term.astype(jnp.bfloat16).astype(jnp.float32)
    k_weight_grad = jnp.dot(inputs.T, raw_low, preferred_element_type=jnp.float32)
    v_weight_grad = jnp.dot(inputs.T, value_low, preferred_element_type=jnp.float32)
    return (inputs_total.astype(jnp.bfloat16), query_grad, k_weight_grad, v_weight_grad)
```

```python
import jax
import jax.numpy as jnp
from jax import lax
from jax.sharding import Mesh, PartitionSpec as P

WIN = 1024
NY, NZ, NX = 4, 8, 2
F32, BF16 = jnp.float32, jnp.bfloat16

score_scale = 168.0 ** (-0.5)


def hop(block, axis, n, step):
    return lax.ppermute(block, axis, [(i, (i + step) % n) for i in range(n)])


def seq_shift(block, distance):
    count = NY * NZ * NX
    route = [(i, i + distance) for i in range(count) if 0 <= i + distance < count]
    return lax.ppermute(block, ("y", "z", "xl"), route)


def ring_gather(block, axis, n, put, buffer, split):
    me = lax.axis_index(axis)
    half = n // 2
    up = down = block
    steps = []
    for t in range(1, half):
        up, down = hop(up, axis, n, 1), hop(down, axis, n, -1)
        steps.append((up, down, t))
    top, bottom = hop(split(up, 0), axis, n, 1), hop(split(down, 1), axis, n, -1)
    buffer = put(buffer, block, me, None)
    for up, down, t in steps:
        buffer = put(buffer, up, lax.rem(me + n - t, n), None)
        buffer = put(buffer, down, lax.rem(me + t, n), None)
    far = lax.rem(me + half, n)
    return put(put(buffer, top, far, 0), bottom, far, 1)


def ring_reduce(own, axis, n, split, join):
    me = lax.axis_index(axis)
    half = n // 2
    far = own(lax.rem(me + half, n))
    up = hop(split(far, 0).astype(BF16), axis, n, 1).astype(F32)
    down = hop(split(far, 1).astype(BF16), axis, n, -1).astype(F32)
    for t in range(2, half + 1):
        ahead = own(lax.rem(me + half - t + 1, n))
        behind = own(lax.rem(me + n - half + t - 1, n))
        if t == 2:
            ahead = join(split(ahead, 0) + up, split(ahead, 1))
            behind = join(split(behind, 0), split(behind, 1) + down)
        else:
            ahead, behind = ahead + up, behind + down
        up = hop(ahead.astype(BF16), axis, n, 1).astype(F32)
        down = hop(behind.astype(BF16), axis, n, -1).astype(F32)
    return own(me) + up + down


def lanes(block, part):
    h = block.shape[-1] // 2
    return block[..., part * h : (part + 1) * h]


def majors(block, part):
    h = block.shape[0] // 2
    return block[part * h : (part + 1) * h]


def take(array, index, axis):
    return lax.dynamic_index_in_dim(array, index, axis, keepdims=False)


def gather_weights(k_weight, v_weight):
    xl = lax.axis_index("xl")
    both = jnp.concatenate([k_weight, v_weight], 1)
    other = hop(both, "xl", NX, 1)
    pair = jnp.where(
        xl == 0, jnp.concatenate([both, other], 0), jnp.concatenate([other, both], 0)
    )
    width = k_weight.shape[1]
    k_pair, v_pair = pair[:, :width], pair[:, width:]
    rows = pair.shape[0]

    def put_small(buffer, block, index, part):
        start = (index, 0, 0 if part is None else part * (width // 2))
        return lax.dynamic_update_slice(buffer, block[None], start)

    def put_z(buffer, block, index, part):
        start = (0 if part is None else part * (NY // 2), index, 0, 0)
        return lax.dynamic_update_slice(buffer, block[:, None], start)

    def put_y(buffer, block, index, part):
        start = (index, 0 if part is None else part * (NZ // 2), 0, 0)
        return lax.dynamic_update_slice(buffer, block[None], start)

    k_y = ring_gather(k_pair, "y", NY, put_small, jnp.zeros((NY, rows, width), BF16), lanes)
    v_z = ring_gather(v_pair, "z", NZ, put_small, jnp.zeros((NZ, rows, width), BF16), lanes)
    full = jnp.zeros((NY, NZ, rows, width), BF16)
    k_full = ring_gather(k_y, "z", NZ, put_z, full, majors)
    v_full = ring_gather(v_z, "y", NY, put_y, full, majors)
    return k_full, v_full


def reduce_pair(block):
    xl = lax.axis_index("xl")
    rows = block.shape[0] // 2
    parts = block.reshape(2, rows, block.shape[1])
    return take(parts, xl, 0) + hop(take(parts, 1 - xl, 0).astype(BF16), "xl", NX, 1).astype(F32)


def join_lanes(a, b):
    return jnp.concatenate([a, b], -1)


def join_majors(a, b):
    return jnp.concatenate([a, b], 0)


def reduce_k(grad):
    grad = grad.reshape(NY, NZ, -1, grad.shape[1])
    over_z = ring_reduce(lambda i: take(grad, i, 1), "z", NZ, majors, join_majors)
    over_y = ring_reduce(lambda i: take(over_z, i, 0), "y", NY, lanes, join_lanes)
    return reduce_pair(over_y)


def reduce_v(grad):
    grad = grad.reshape(NY, NZ, -1, grad.shape[1])
    over_y = ring_reduce(lambda i: take(grad, i, 0), "y", NY, majors, join_majors)
    over_z = ring_reduce(lambda i: take(over_y, i, 0), "z", NZ, lanes, join_lanes)
    return reduce_pair(over_z)


def per_device(inputs, queries, out_grad, segment_ids, k_weight, v_weight, k_gain):
    tok_rows = inputs.shape[0]
    head_dim = queries.shape[2]
    width = k_weight.shape[1]
    kv_local = width // head_dim
    group_size = queries.shape[1] // kv_local
    seq_index = lax.axis_index(("y", "z", "xl"))
    row_base = seq_index * tok_rows
    local_pos = row_base + jnp.arange(tok_rows, dtype=jnp.int32)
    k_full, v_full = gather_weights(k_weight, v_weight)
    seg_one, seg_two = seq_shift(segment_ids, 1), seq_shift(segment_ids, 2)
    key_seg = jnp.concatenate([seg_two, seg_one, segment_ids], 0)

    k_raw = jnp.dot(inputs, k_full.reshape(-1, width), preferred_element_type=F32)
    k_raw = k_raw.reshape(tok_rows, kv_local, head_dim)
    k_inv = lax.rsqrt(jnp.mean(k_raw * k_raw, axis=-1, keepdims=True) + 1e-06)
    k_normed = k_raw * k_inv
    keys_own = (k_normed * k_gain).astype(BF16).reshape(tok_rows, width)
    keys_one, keys_two = seq_shift(keys_own, 1), seq_shift(keys_own, 2)
    v_raw = jnp.dot(inputs, v_full.reshape(-1, width), preferred_element_type=F32)
    values_own = v_raw.astype(BF16)
    values_one, values_two = seq_shift(values_own, 1), seq_shift(values_own, 2)

    key_block = jnp.concatenate([keys_two, keys_one, keys_own], 0).reshape(-1, kv_local, head_dim)
    value_block = jnp.concatenate([values_two, values_one, values_own], 0).reshape(
        -1, kv_local, head_dim
    )
    key_pos = row_base - 2 * tok_rows + jnp.arange(3 * tok_rows, dtype=jnp.int32)
    query_view = queries.reshape(tok_rows, kv_local, group_size, head_dim)
    grad_view = out_grad.reshape(tok_rows, kv_local, group_size, head_dim)
    distance = local_pos[:, None] - key_pos[None, :]
    allowed = (
        (distance >= 0)
        & (distance < WIN)
        & (segment_ids[:, None] == key_seg[None, :])
        & (key_pos[None, :] >= 0)
    )
    scores = (
        jnp.einsum("qkgd,ckd->kgqc", query_view, key_block, preferred_element_type=F32)
        * score_scale
    )
    scores = jnp.where(allowed[None, None], scores, -1e30)
    row_peak = jnp.max(scores, axis=-1, keepdims=True)
    log_total = row_peak[..., 0] + jnp.log(jnp.sum(jnp.exp(scores - row_peak), axis=-1))
    probs = jnp.exp(scores - log_total[..., None])
    probs_low = probs.astype(BF16)
    attn_out = jnp.einsum("kgqc,ckd->qkgd", probs_low, value_block, preferred_element_type=F32)
    delta = jnp.transpose(jnp.sum(grad_view.astype(F32) * attn_out, axis=-1), (1, 2, 0))
    prob_grad = jnp.einsum("qkgd,ckd->kgqc", grad_view, value_block, preferred_element_type=F32)
    score_grad = (probs * (prob_grad - delta[..., None])).astype(BF16)
    query_grad = (
        jnp.einsum("kgqc,ckd->qkgd", score_grad, key_block, preferred_element_type=F32)
        * score_scale
    )
    key_all = (
        jnp.einsum("kgqc,qkgd->ckd", score_grad, query_view, preferred_element_type=F32)
        * score_scale
    ).reshape(-1, width)
    value_all = jnp.einsum(
        "kgqc,qkgd->ckd", probs_low, grad_view, preferred_element_type=F32
    ).reshape(-1, width)

    def collect(grads):
        low = grads[: 2 * tok_rows].astype(BF16)
        one, two = seq_shift(low[tok_rows:], -1), seq_shift(low[:tok_rows], -2)
        return grads[2 * tok_rows :] + one.astype(F32) + two.astype(F32)

    value_low = collect(value_all).astype(BF16)
    key_grad = collect(key_all).reshape(tok_rows, kv_local, head_dim)
    normed_grad = key_grad * k_gain
    raw_grad = (
        normed_grad - k_normed * jnp.mean(normed_grad * k_normed, axis=-1, keepdims=True)
    ) * k_inv
    raw_low = raw_grad.astype(BF16).reshape(tok_rows, width)

    def weight_grad(low):
        return lax.dot_general(inputs, low, (((0,), (0,)), ((), ())), preferred_element_type=F32)

    v_weight_grad = reduce_v(weight_grad(value_low))
    k_weight_grad = reduce_k(weight_grad(raw_low))

    xh, core = lax.axis_index("xh"), lax.axis_index("c")
    k_quarters = k_full.reshape(2, 2, -1, width)
    v_quarters = v_full.reshape(2, 2, -1, width)

    def input_term(k_part, v_part):
        dims = (((1,), (1,)), ((), ()))
        return lax.dot_general(raw_low, k_part, dims, preferred_element_type=F32) + lax.dot_general(
            value_low, v_part, dims, preferred_element_type=F32
        )

    def for_core(which):
        k_half = take(k_quarters, which, 1)
        v_half = take(v_quarters, which, 1)
        return [input_term(take(k_half, i, 0), take(v_half, i, 0)) for i in (1 - xh, xh)]

    away = [hop(t.astype(BF16), "c", 2, 1).astype(F32) for t in for_core(1 - core)]
    far, near = [t + a for t, a in zip(for_core(core), away)]
    inputs_grad = (near + hop(far.astype(BF16), "xh", 2, 1).astype(F32)).astype(BF16)
    return (
        inputs_grad,
        query_grad.astype(BF16).reshape(tok_rows, kv_local * group_size, head_dim),
        k_weight_grad,
        v_weight_grad,
    )


def solution(mesh):
    fine = Mesh(mesh.devices.reshape(NY, NZ, NX, 2, 2), ("y", "z", "xl", "xh", "c"))
    seq, head = ("y", "z", "xl"), ("xh", "c")
    in_specs = (
        P(seq, None),
        P(seq, head, None),
        P(seq, head, None),
        P(seq),
        P(seq, head),
        P(seq, head),
        P(),
    )
    out_specs = (P(seq, head), P(seq, head, None), P(seq, head), P(seq, head))
    return jax.shard_map(
        per_device, mesh=fine, in_specs=in_specs, out_specs=out_specs, check_vma=False
    )
```

```python
import jax
import jax.numpy as jnp
from jax import lax
from jax.experimental import pallas as pl
from jax.experimental.pallas import tpu as pltpu
from jax.sharding import Mesh, PartitionSpec as P

WIN = 1024
NY, NZ, NX = 4, 8, 2
F32, BF16 = jnp.float32, jnp.bfloat16

score_scale = 168.0 ** (-0.5)


def hop(block, axis, n, step):
    return lax.ppermute(block, axis, [(i, (i + step) % n) for i in range(n)])


def seq_shift(block, distance):
    count = NY * NZ * NX
    route = [(i, i + distance) for i in range(count) if 0 <= i + distance < count]
    return lax.ppermute(block, ("y", "z", "xl"), route)


def ring_gather(block, axis, n, put, buffer, split):
    me = lax.axis_index(axis)
    half = n // 2
    up = down = block
    steps = []
    for t in range(1, half):
        up, down = hop(up, axis, n, 1), hop(down, axis, n, -1)
        steps.append((up, down, t))
    top, bottom = hop(split(up, 0), axis, n, 1), hop(split(down, 1), axis, n, -1)
    buffer = put(buffer, block, me, None)
    for up, down, t in steps:
        buffer = put(buffer, up, lax.rem(me + n - t, n), None)
        buffer = put(buffer, down, lax.rem(me + t, n), None)
    far = lax.rem(me + half, n)
    return put(put(buffer, top, far, 0), bottom, far, 1)


def ring_reduce(own, axis, n, split, join):
    me = lax.axis_index(axis)
    half = n // 2
    far = own(lax.rem(me + half, n))
    up = hop(split(far, 0).astype(BF16), axis, n, 1).astype(F32)
    down = hop(split(far, 1).astype(BF16), axis, n, -1).astype(F32)
    for t in range(2, half + 1):
        ahead = own(lax.rem(me + half - t + 1, n))
        behind = own(lax.rem(me + n - half + t - 1, n))
        if t == 2:
            ahead = join(split(ahead, 0) + up, split(ahead, 1))
            behind = join(split(behind, 0), split(behind, 1) + down)
        else:
            ahead, behind = ahead + up, behind + down
        up = hop(ahead.astype(BF16), axis, n, 1).astype(F32)
        down = hop(behind.astype(BF16), axis, n, -1).astype(F32)
    return own(me) + up + down


def majors(block, part):
    h = block.shape[0] // 2
    return block[part * h : (part + 1) * h]


def take(array, index, axis):
    return lax.dynamic_index_in_dim(array, index, axis, keepdims=False)


def exchange(blocks, axes):
    return lax.all_to_all(blocks, axes, split_axis=0, concat_axis=0, tiled=True)


def gather(block, axes, n):
    return exchange(jnp.broadcast_to(block[None], (n, *block.shape)), axes)


def gather_first(shard, full):
    rows, width = shard.shape
    near = gather(shard, ("y", "xl"), NY * NX).reshape(NY, NX * rows, width)

    def put(buffer, block, index, part):
        start = (0 if part is None else part * (NY // 2), index, 0, 0)
        return lax.dynamic_update_slice(buffer, block[:, None], start)

    return ring_gather(near, "z", NZ, put, full, majors)


def gather_second(shard):
    rows, width = shard.shape
    near = gather(shard, ("z", "xl"), NZ * NX).reshape(NZ * NX * rows, width)
    return gather(near, "y", NY)


def total(blocks):
    return jnp.sum(blocks.astype(F32), axis=0)


def reduce_first(grad):
    grad = grad.reshape(NY, NZ, -1, grad.shape[1])
    over_z = ring_reduce(lambda i: take(grad, i, 1), "z", NZ, majors, join_majors)
    low = over_z.astype(BF16).reshape(NY * NX, -1, grad.shape[-1])
    return total(exchange(low, ("y", "xl")))


def reduce_second(grad):
    low = grad.astype(BF16).reshape(NY, -1, grad.shape[1])
    over_y = total(exchange(low, "y"))
    low = over_y.astype(BF16).reshape(NZ * NX, -1, grad.shape[1])
    return total(exchange(low, ("z", "xl")))


def join_majors(a, b):
    return jnp.concatenate([a, b], 0)


QB, KB = 256, 256
DOT_ROWS = (((1,), (1,)), ((), ()))
LOG2E = 1.4426950408889634


def attention_kernel(
    q_ref, do_ref, two_ref, one_ref, own_ref, qseg_ref, kseg_ref,
    dq_ref, back_ref, mine_ref, kv, s_buf, dp_buf, ds_buf, acc
):
    tok = q_ref.shape[0]
    hd = q_ref.shape[1] // 2
    span = WIN + QB
    step = pl.program_id(0)

    @pl.when(step == 0)
    def _():
        kv[0:tok] = two_ref[...]
        kv[tok : 2 * tok] = one_ref[...]
        kv[2 * tok :] = own_ref[...]
        acc[...] = jnp.zeros_like(acc)

    base = pl.multiple_of(step * QB, QB)
    q_rows = pl.ds(base, QB)
    q = jnp.concatenate([q_ref[q_rows, :hd], q_ref[q_rows, hd:]], 0)
    do = jnp.concatenate([do_ref[q_rows, :hd], do_ref[q_rows, hd:]], 0)
    qseg = qseg_ref[step]
    peak = jnp.full((8, 2 * QB), -1e30, F32)
    chunks = range(0, span, KB)
    r_minus_c = lax.broadcasted_iota(jnp.int32, (KB, QB), 1) - lax.broadcasted_iota(
        jnp.int32, (KB, QB), 0
    )
    for c in chunks:
        rows = pl.ds(pl.multiple_of(base + c, KB), KB)
        s = lax.dot_general(kv[rows, :hd], q, DOT_ROWS, preferred_element_type=F32)
        kseg = kseg_ref[rows, :]
        kseg = jnp.concatenate([kseg] * (QB // kseg.shape[1]), 1)
        ok = kseg == qseg
        if c < QB:
            ok = ok & (r_minus_c < c)
        if c + KB > WIN:
            ok = ok & (r_minus_c >= c - WIN)
        s = jnp.where(jnp.concatenate([ok, ok], 1), s * (score_scale * LOG2E), -1e30)
        s_buf[c : c + KB] = s
        peak = jnp.maximum(peak, jnp.max(s.reshape(KB // 8, 8, 2 * QB), axis=0))
        dp_buf[c : c + KB] = lax.dot_general(
            kv[rows, hd:], do, DOT_ROWS, preferred_element_type=F32
        )
    peak = jnp.max(peak, axis=0, keepdims=True)
    denom = jnp.zeros((8, 2 * QB), F32)
    for c in chunks:
        p = jnp.exp2(s_buf[c : c + KB] - peak)
        s_buf[c : c + KB] = p
        denom = denom + jnp.sum(p.reshape(KB // 8, 8, 2 * QB), axis=0)
    inverse = 1.0 / jnp.sum(denom, axis=0, keepdims=True)
    delta = jnp.zeros((8, 2 * QB), F32)
    for c in chunks:
        rows = pl.ds(pl.multiple_of(base + c, KB), KB)
        p = s_buf[c : c + KB] * inverse
        s_buf[c : c + KB] = p
        low = p.astype(BF16)
        acc[rows, hd:] += jnp.dot(low, do, preferred_element_type=F32)
        part = low.astype(F32) * dp_buf[c : c + KB]
        delta = delta + jnp.sum(part.reshape(KB // 8, 8, 2 * QB), axis=0)
    delta = jnp.sum(delta, axis=0, keepdims=True)
    for c in chunks:
        rows = pl.ds(pl.multiple_of(base + c, KB), KB)
        ds = (s_buf[c : c + KB] * (dp_buf[c : c + KB] - delta)).astype(BF16)
        ds_buf[c : c + KB] = ds
        acc[rows, :hd] += jnp.dot(ds, q, preferred_element_type=F32)
    k_turned = kv[pl.ds(base, span), :hd].T
    dq = jnp.dot(k_turned, ds_buf[...], preferred_element_type=F32) * score_scale
    dq = dq.T.astype(BF16)
    dq_ref[q_rows, :hd] = dq[:QB]
    dq_ref[q_rows, hd:] = dq[QB:]

    @pl.when(step == pl.num_programs(0) - 1)
    def _():
        back_ref[:, :hd] = (acc[: 2 * tok, :hd] * score_scale).astype(BF16)
        back_ref[:, hd:] = acc[: 2 * tok, hd:].astype(BF16)
        mine_ref[:, :hd] = acc[2 * tok :, :hd] * score_scale
        mine_ref[:, hd:] = acc[2 * tok :, hd:]


def attention(q, do, kv_two, kv_one, kv_own, qseg, kseg):
    tok, width = q.shape
    span = WIN + QB
    whole = pl.BlockSpec(memory_space=pltpu.VMEM)
    flops = 10 * (2 * tok) * span * (width // 2)
    return pl.pallas_call(
        attention_kernel,
        grid=(tok // QB,),
        in_specs=[whole] * 7,
        out_specs=[whole] * 3,
        out_shape=[
            jax.ShapeDtypeStruct((tok, width), BF16),
            jax.ShapeDtypeStruct((2 * tok, width), BF16),
            jax.ShapeDtypeStruct((tok, width), F32),
        ],
        scratch_shapes=[
            pltpu.VMEM((3 * tok, width), BF16),
            pltpu.VMEM((span, 2 * QB), F32),
            pltpu.VMEM((span, 2 * QB), F32),
            pltpu.VMEM((span, 2 * QB), BF16),
            pltpu.VMEM((3 * tok, width), F32),
        ],
        compiler_params=pltpu.CompilerParams(vmem_limit_bytes=24 << 20),
        cost_estimate=pl.CostEstimate(
            flops=flops, bytes_accessed=8 << 20, transcendentals=2 * tok * span
        ),
    )(q, do, kv_two, kv_one, kv_own, qseg, kseg)


def weight_grad_kernel(x_ref, g_ref, o_ref):
    o_ref[...] = jnp.dot(x_ref[...], g_ref[...], preferred_element_type=F32)


def weight_grad(inputs_turned, grads):
    depth, tok = inputs_turned.shape
    width = grads.shape[1]
    block = depth // 8
    return pl.pallas_call(
        weight_grad_kernel,
        grid=(8,),
        in_specs=[
            pl.BlockSpec((block, tok), lambda i: (i, 0)),
            pl.BlockSpec((tok, width), lambda i: (0, 0)),
        ],
        out_specs=pl.BlockSpec((block, width), lambda i: (i, 0)),
        out_shape=jax.ShapeDtypeStruct((depth, width), F32),
        compiler_params=pltpu.CompilerParams(vmem_limit_bytes=16 << 20),
        cost_estimate=pl.CostEstimate(
            flops=2 * depth * tok * width, bytes_accessed=12 << 20, transcendentals=0
        ),
    )(inputs_turned, grads)


def per_device(inputs, queries, out_grad, segment_ids, k_weight, v_weight, k_gain):
    tok, depth = inputs.shape
    hd = queries.shape[2]
    heads = queries.shape[1]
    seq_index = lax.axis_index(("y", "z", "xl"))

    def shard(g):
        cols = slice(g * hd, (g + 1) * hd)
        return jnp.concatenate([k_weight[:, cols], v_weight[:, cols]], 1)

    rows = k_weight.shape[0]
    full = jnp.zeros((NY, NZ, NX * rows, 2 * hd), BF16)
    weights = [
        gather_first(shard(0), full).reshape(depth, 2 * hd),
        gather_second(shard(1)).reshape(depth, 2 * hd),
    ]
    inputs_turned = inputs.T
    seg_one, seg_two = seq_shift(segment_ids, 1), seq_shift(segment_ids, 2)
    key_seg = jnp.concatenate(
        [
            jnp.where(seq_index >= 2, seg_two, -1),
            jnp.where(seq_index >= 1, seg_one, -1),
            segment_ids,
        ],
        0,
    )
    key_seg = jnp.broadcast_to(key_seg[:, None], (3 * tok, 128))
    query_seg = segment_ids.reshape(tok // QB, 1, QB)
    q_flat = queries.reshape(tok, heads * hd)
    do_flat = out_grad.reshape(tok, heads * hd)

    def forward(weight):
        raw = jnp.dot(inputs, weight, preferred_element_type=F32)
        k_raw = raw[:, :hd]
        k_inv = lax.rsqrt(jnp.mean(k_raw * k_raw, axis=-1, keepdims=True) + 1e-06)
        k_normed = k_raw * k_inv
        own = jnp.concatenate([k_normed * k_gain, raw[:, hd:]], 1).astype(BF16)
        return own, k_normed, k_inv

    def backward(own, k_normed, k_inv, g):
        cols = slice(2 * g * hd, 2 * (g + 1) * hd)
        one, two = seq_shift(own, 1), seq_shift(own, 2)
        dq, back, mine = attention(
            q_flat[:, cols], do_flat[:, cols], two, one, own, query_seg, key_seg
        )
        grads = (
            mine
            + seq_shift(back[tok:], -1).astype(F32)
            + seq_shift(back[:tok], -2).astype(F32)
        )
        normed_grad = grads[:, :hd] * k_gain
        raw_grad = (
            normed_grad - k_normed * jnp.mean(normed_grad * k_normed, axis=-1, keepdims=True)
        ) * k_inv
        return dq, jnp.concatenate([raw_grad, grads[:, hd:]], 1).astype(BF16)

    state = [forward(w) for w in weights]
    dqs, lows = zip(*[backward(*state[g], g) for g in (0, 1)])
    query_grad = jnp.concatenate(dqs, 1).reshape(tok, heads, hd)

    sums = [
        reduce_first(weight_grad(inputs_turned, lows[0])),
        reduce_second(weight_grad(inputs_turned, lows[1])),
    ]
    k_weight_grad = jnp.concatenate([s[:, :hd] for s in sums], 1)
    v_weight_grad = jnp.concatenate([s[:, hd:] for s in sums], 1)

    xh, core = lax.axis_index("xh"), lax.axis_index("c")
    quarters = [w.reshape(2, 2, -1, 2 * hd) for w in weights]

    def for_core(which):
        halves = [take(q, which, 1) for q in quarters]
        return [
            sum(
                lax.dot_general(low, take(h, i, 0), DOT_ROWS, preferred_element_type=F32)
                for low, h in zip(lows, halves)
            )
            for i in (1 - xh, xh)
        ]

    away = [hop(t.astype(BF16), "c", 2, 1).astype(F32) for t in for_core(1 - core)]
    far, near = [t + a for t, a in zip(for_core(core), away)]
    inputs_grad = (near + hop(far.astype(BF16), "xh", 2, 1).astype(F32)).astype(BF16)
    return inputs_grad, query_grad, k_weight_grad, v_weight_grad


def solution(mesh):
    fine = Mesh(mesh.devices.reshape(NY, NZ, NX, 2, 2), ("y", "z", "xl", "xh", "c"))
    seq, head = ("y", "z", "xl"), ("xh", "c")
    in_specs = (
        P(seq, None),
        P(seq, head, None),
        P(seq, head, None),
        P(seq),
        P(seq, head),
        P(seq, head),
        P(),
    )
    out_specs = (P(seq, head), P(seq, head, None), P(seq, head), P(seq, head))
    return jax.shard_map(
        per_device, mesh=fine, in_specs=in_specs, out_specs=out_specs, check_vma=False
    )
```

```python
import jax
import jax.numpy as jnp
from jax import lax
from jax.experimental import pallas as pl
from jax.experimental.pallas import tpu as pltpu
from jax.sharding import Mesh, PartitionSpec as P

WIN = 1024
NY, NZ, NX = 4, 8, 2
F32, BF16 = jnp.float32, jnp.bfloat16

score_scale = 168.0 ** (-0.5)


def hop(block, axis, n, step):
    return lax.ppermute(block, axis, [(i, (i + step) % n) for i in range(n)])


def seq_shift(block, distance):
    count = NY * NZ * NX
    route = [(i, i + distance) for i in range(count) if 0 <= i + distance < count]
    return lax.ppermute(block, ("y", "z", "xl"), route)


def ring_gather(block, axis, n, put, buffer, split):
    me = lax.axis_index(axis)
    half = n // 2
    up = down = block
    steps = []
    for t in range(1, half):
        up, down = hop(up, axis, n, 1), hop(down, axis, n, -1)
        steps.append((up, down, t))
    top, bottom = hop(split(up, 0), axis, n, 1), hop(split(down, 1), axis, n, -1)
    buffer = put(buffer, block, me, None)
    for up, down, t in steps:
        buffer = put(buffer, up, lax.rem(me + n - t, n), None)
        buffer = put(buffer, down, lax.rem(me + t, n), None)
    far = lax.rem(me + half, n)
    return put(put(buffer, top, far, 0), bottom, far, 1)


def ring_reduce(own, axis, n, split, join):
    me = lax.axis_index(axis)
    half = n // 2
    far = own(lax.rem(me + half, n))
    up = hop(split(far, 0).astype(BF16), axis, n, 1).astype(F32)
    down = hop(split(far, 1).astype(BF16), axis, n, -1).astype(F32)
    for t in range(2, half + 1):
        ahead = own(lax.rem(me + half - t + 1, n))
        behind = own(lax.rem(me + n - half + t - 1, n))
        if t == 2:
            ahead = join(split(ahead, 0) + up, split(ahead, 1))
            behind = join(split(behind, 0), split(behind, 1) + down)
        else:
            ahead, behind = ahead + up, behind + down
        up = hop(ahead.astype(BF16), axis, n, 1).astype(F32)
        down = hop(behind.astype(BF16), axis, n, -1).astype(F32)
    return own(me) + up + down


def majors(block, part):
    h = block.shape[0] // 2
    return block[part * h : (part + 1) * h]


def take(array, index, axis):
    return lax.dynamic_index_in_dim(array, index, axis, keepdims=False)


def join_majors(a, b):
    return jnp.concatenate([a, b], 0)


def lanes(block, part):
    h = block.shape[-1] // 2
    return block[..., part * h : (part + 1) * h]


def join_lanes(a, b):
    return jnp.concatenate([a, b], -1)


def put_block(buffer, block, index, part):
    start = (index, 0, 0 if part is None else part * (buffer.shape[-1] // 2))
    return lax.dynamic_update_slice(buffer, block[None], start)


def put_strip(buffer, block, index, part):
    start = (0 if part is None else part * (buffer.shape[0] // 2), index, 0, 0)
    return lax.dynamic_update_slice(buffer, block[:, None], start)


def gather_half(shard, xl):
    other = hop(shard, "xl", NX, 1)
    pair = jnp.where(xl == 0, join_majors(shard, other), join_majors(other, shard))
    rows, width = pair.shape
    blocks = ring_gather(pair, "y", NY, put_block, jnp.zeros((NY, rows, width), BF16), lanes)
    near = jnp.where(xl == 0, blocks[: NY // 2], blocks[NY // 2 :])
    full = jnp.zeros((NY // 2, NZ, rows, width), BF16)
    return near, lambda near: ring_gather(near, "z", NZ, put_strip, full, majors).reshape(-1, width)


def reduce_half(grad, xl):
    width = grad.shape[1]
    grad = grad.reshape(NY // 2, NZ, -1, width)
    over_z = ring_reduce(lambda i: take(grad, i, 1), "z", NZ, majors, join_majors)
    none = jnp.zeros_like(over_z)
    blocks = jnp.where(xl == 0, join_majors(over_z, none), join_majors(none, over_z))
    over_y = ring_reduce(lambda i: take(blocks, i, 0), "y", NY, lanes, join_lanes)
    parts = over_y.reshape(NX, -1, width)
    away = hop(take(parts, 1 - xl, 0).astype(BF16), "xl", NX, 1)
    return take(parts, xl, 0) + away.astype(F32)


QB, KB = 256, 256
DOT_ROWS = (((1,), (1,)), ((), ()))
LOG2E = 1.4426950408889634


def attention_kernel(
    q_ref, do_ref, two_ref, one_ref, own_ref, qseg_ref, kseg_ref,
    dq_ref, back_ref, mine_ref, kv, s_buf, dp_buf, ds_buf, acc
):
    tok = q_ref.shape[0]
    hd = q_ref.shape[1] // 2
    span = WIN + QB
    step = pl.program_id(0)

    @pl.when(step == 0)
    def _():
        kv[0:tok] = two_ref[...]
        kv[tok : 2 * tok] = one_ref[...]
        kv[2 * tok :] = own_ref[...]
        acc[...] = jnp.zeros_like(acc)

    base = pl.multiple_of(step * QB, QB)
    q_rows = pl.ds(base, QB)
    q = jnp.concatenate([q_ref[q_rows, :hd], q_ref[q_rows, hd:]], 0)
    do = jnp.concatenate([do_ref[q_rows, :hd], do_ref[q_rows, hd:]], 0)
    qseg = qseg_ref[step]
    peak = jnp.full((8, 2 * QB), -1e30, F32)
    chunks = range(0, span, KB)
    r_minus_c = lax.broadcasted_iota(jnp.int32, (KB, QB), 1) - lax.broadcasted_iota(
        jnp.int32, (KB, QB), 0
    )
    for c in chunks:
        rows = pl.ds(pl.multiple_of(base + c, KB), KB)
        s = lax.dot_general(kv[rows, :hd], q, DOT_ROWS, preferred_element_type=F32)
        kseg = kseg_ref[rows, :]
        kseg = jnp.concatenate([kseg] * (QB // kseg.shape[1]), 1)
        ok = kseg == qseg
        if c < QB:
            ok = ok & (r_minus_c < c)
        if c + KB > WIN:
            ok = ok & (r_minus_c >= c - WIN)
        s = jnp.where(jnp.concatenate([ok, ok], 1), s * (score_scale * LOG2E), -1e30)
        s_buf[c : c + KB] = s
        peak = jnp.maximum(peak, jnp.max(s.reshape(KB // 8, 8, 2 * QB), axis=0))
        dp_buf[c : c + KB] = lax.dot_general(
            kv[rows, hd:], do, DOT_ROWS, preferred_element_type=F32
        )
    peak = jnp.max(peak, axis=0, keepdims=True)
    denom = jnp.zeros((8, 2 * QB), F32)
    for c in chunks:
        p = jnp.exp2(s_buf[c : c + KB] - peak)
        s_buf[c : c + KB] = p
        denom = denom + jnp.sum(p.reshape(KB // 8, 8, 2 * QB), axis=0)
    inverse = 1.0 / jnp.sum(denom, axis=0, keepdims=True)
    delta = jnp.zeros((8, 2 * QB), F32)
    for c in chunks:
        rows = pl.ds(pl.multiple_of(base + c, KB), KB)
        p = s_buf[c : c + KB] * inverse
        s_buf[c : c + KB] = p
        low = p.astype(BF16)
        acc[rows, hd:] += jnp.dot(low, do, preferred_element_type=F32)
        part = low.astype(F32) * dp_buf[c : c + KB]
        delta = delta + jnp.sum(part.reshape(KB // 8, 8, 2 * QB), axis=0)
    delta = jnp.sum(delta, axis=0, keepdims=True)
    for c in chunks:
        rows = pl.ds(pl.multiple_of(base + c, KB), KB)
        ds = (s_buf[c : c + KB] * (dp_buf[c : c + KB] - delta)).astype(BF16)
        ds_buf[c : c + KB] = ds
        acc[rows, :hd] += jnp.dot(ds, q, preferred_element_type=F32)
    k_turned = kv[pl.ds(base, span), :hd].T
    dq = jnp.dot(k_turned, ds_buf[...], preferred_element_type=F32) * score_scale
    dq = dq.T.astype(BF16)
    dq_ref[q_rows, :hd] = dq[:QB]
    dq_ref[q_rows, hd:] = dq[QB:]

    @pl.when(step == pl.num_programs(0) - 1)
    def _():
        back_ref[:, :hd] = (acc[: 2 * tok, :hd] * score_scale).astype(BF16)
        back_ref[:, hd:] = acc[: 2 * tok, hd:].astype(BF16)
        mine_ref[:, :hd] = acc[2 * tok :, :hd] * score_scale
        mine_ref[:, hd:] = acc[2 * tok :, hd:]


def attention(q, do, kv_two, kv_one, kv_own, qseg, kseg):
    tok, width = q.shape
    span = WIN + QB
    whole = pl.BlockSpec(memory_space=pltpu.VMEM)
    flops = 10 * (2 * tok) * span * (width // 2)
    return pl.pallas_call(
        attention_kernel,
        grid=(tok // QB,),
        in_specs=[whole] * 7,
        out_specs=[whole] * 3,
        out_shape=[
            jax.ShapeDtypeStruct((tok, width), BF16),
            jax.ShapeDtypeStruct((2 * tok, width), BF16),
            jax.ShapeDtypeStruct((tok, width), F32),
        ],
        scratch_shapes=[
            pltpu.VMEM((3 * tok, width), BF16),
            pltpu.VMEM((span, 2 * QB), F32),
            pltpu.VMEM((span, 2 * QB), F32),
            pltpu.VMEM((span, 2 * QB), BF16),
            pltpu.VMEM((3 * tok, width), F32),
        ],
        compiler_params=pltpu.CompilerParams(vmem_limit_bytes=24 << 20),
        cost_estimate=pl.CostEstimate(
            flops=flops, bytes_accessed=8 << 20, transcendentals=2 * tok * span
        ),
    )(q, do, kv_two, kv_one, kv_own, qseg, kseg)


def weight_grad_kernel(own_ref, par_ref, g_ref, h_ref, o_ref):
    o_ref[...] = jnp.dot(own_ref[...], g_ref[...], preferred_element_type=F32) + jnp.dot(
        par_ref[...], h_ref[...], preferred_element_type=F32
    )


def weight_grad(own_turned, par_turned, own_grads, par_grads):
    depth, tok = own_turned.shape
    width = own_grads.shape[1]
    block = depth // 8
    left = pl.BlockSpec((block, tok), lambda i: (i, 0))
    right = pl.BlockSpec((tok, width), lambda i: (0, 0))
    return pl.pallas_call(
        weight_grad_kernel,
        grid=(8,),
        in_specs=[left, left, right, right],
        out_specs=pl.BlockSpec((block, width), lambda i: (i, 0)),
        out_shape=jax.ShapeDtypeStruct((depth, width), F32),
        compiler_params=pltpu.CompilerParams(vmem_limit_bytes=16 << 20),
        cost_estimate=pl.CostEstimate(
            flops=4 * depth * tok * width, bytes_accessed=12 << 20, transcendentals=0
        ),
    )(own_turned, par_turned, own_grads, par_grads)


def per_device(inputs, queries, out_grad, segment_ids, k_weight, v_weight, k_gain):
    tok, depth = inputs.shape
    hd = queries.shape[2]
    heads = queries.shape[1]
    groups = k_weight.shape[1] // hd
    seq_index = lax.axis_index(("y", "z", "xl"))
    xl, xh, core = lax.axis_index("xl"), lax.axis_index("xh"), lax.axis_index("c")

    def group(g):
        return slice(2 * g * hd, 2 * (g + 1) * hd)

    shard = jnp.concatenate(
        [w[:, g * hd : (g + 1) * hd] for g in range(groups) for w in (k_weight, v_weight)], 1
    )
    half = depth // 2
    own_in = jnp.where(xl == 0, inputs[:, :half], inputs[:, half:])
    some = take(inputs.reshape(2, tok // 2, depth), core, 0)
    some = hop(jnp.where(xl == 0, some[:, half:], some[:, :half]), "xl", NX, 1)
    rest = hop(some, "c", 2, 1)
    par_in = jnp.where(core == 0, join_majors(some, rest), join_majors(rest, some))
    near, gather_rest = gather_half(shard, xl)
    near, seg = lax.optimization_barrier((near, segment_ids))
    weight = gather_rest(near)
    own_turned, par_turned = own_in.T, par_in.T

    seg_one, seg_two = seq_shift(seg, 1), seq_shift(seg, 2)
    key_seg = jnp.concatenate(
        [
            jnp.where(seq_index >= 2, seg_two, -1),
            jnp.where(seq_index >= 1, seg_one, -1),
            segment_ids,
        ],
        0,
    )
    key_seg = jnp.broadcast_to(key_seg[:, None], (3 * tok, 128))
    query_seg = segment_ids.reshape(tok // QB, 1, QB)
    q_flat = queries.reshape(tok, heads * hd)
    do_flat = out_grad.reshape(tok, heads * hd)

    par_raw = jnp.dot(par_in, weight, preferred_element_type=F32)
    from_par = [hop(par_raw[:, group(g)], "xl", NX, 1) for g in range(groups)]
    own_raw = jnp.dot(own_in, weight, preferred_element_type=F32)

    def forward(g):
        raw = own_raw[:, group(g)] + from_par[g]
        k_raw = raw[:, :hd]
        k_inv = lax.rsqrt(jnp.mean(k_raw * k_raw, axis=-1, keepdims=True) + 1e-06)
        k_normed = k_raw * k_inv
        own = jnp.concatenate([k_normed * k_gain, raw[:, hd:]], 1).astype(BF16)
        return own, k_normed, k_inv

    def backward(own, k_normed, k_inv, g):
        one, two = seq_shift(own, 1), seq_shift(own, 2)
        dq, back, mine = attention(
            q_flat[:, group(g)], do_flat[:, group(g)], two, one, own, query_seg, key_seg
        )
        grads = (
            mine
            + seq_shift(back[tok:], -1).astype(F32)
            + seq_shift(back[:tok], -2).astype(F32)
        )
        normed_grad = grads[:, :hd] * k_gain
        raw_grad = (
            normed_grad - k_normed * jnp.mean(normed_grad * k_normed, axis=-1, keepdims=True)
        ) * k_inv
        low = jnp.concatenate([raw_grad, grads[:, hd:]], 1).astype(BF16)
        return dq, low, hop(low, "xl", NX, 1)

    state = [forward(g) for g in range(groups)]
    dqs, lows, pars = zip(*[backward(*state[g], g) for g in range(groups)])
    query_grad = jnp.concatenate(dqs, 1).reshape(tok, heads, hd)
    own_grads, par_grads = jnp.concatenate(lows, 1), jnp.concatenate(pars, 1)

    grad = reduce_half(weight_grad(own_turned, par_turned, own_grads, par_grads), xl)
    cols = [grad[:, i * hd : (i + 1) * hd] for i in range(2 * groups)]
    k_weight_grad = jnp.concatenate(cols[0::2], 1)
    v_weight_grad = jnp.concatenate(cols[1::2], 1)

    quarters = weight.reshape(2, half // 2, -1)
    all_grads = jnp.concatenate([own_grads, par_grads], 0)

    def term(which):
        part = take(quarters, which, 0)
        return lax.dot_general(all_grads, part, DOT_ROWS, preferred_element_type=F32)

    away = hop(term(1 - core).astype(BF16), "c", 2, 1)
    summed = term(core) + away.astype(F32)
    own_part, par_part = summed[:tok], summed[tok:]
    keep = xh == xl
    first = lax.ppermute(
        jnp.where(keep, par_part, own_part).astype(BF16),
        ("xl", "xh"),
        [(0, 2), (3, 1), (1, 0), (2, 3)],
    )
    second = lax.ppermute(par_part.astype(BF16), ("xl", "xh"), [(1, 2), (2, 1)])
    inputs_grad = jnp.where(keep, own_part, second.astype(F32)) + first.astype(F32)
    return inputs_grad.astype(BF16), query_grad, k_weight_grad, v_weight_grad


def solution(mesh):
    fine = Mesh(mesh.devices.reshape(NY, NZ, NX, 2, 2), ("y", "z", "xl", "xh", "c"))
    seq, head = ("y", "z", "xl"), ("xh", "c")
    in_specs = (
        P(seq, None),
        P(seq, head, None),
        P(seq, head, None),
        P(seq),
        P(seq, head),
        P(seq, head),
        P(),
    )
    out_specs = (P(seq, head), P(seq, head, None), P(seq, head), P(seq, head))
    return jax.shard_map(
        per_device, mesh=fine, in_specs=in_specs, out_specs=out_specs, check_vma=False
    )
```

```python
import jax
import jax.numpy as jnp
from jax import lax
from jax.experimental import pallas as pl
from jax.experimental.pallas import tpu as pltpu
from jax.sharding import Mesh, PartitionSpec as P

WIN = 1024
NY, NZ, NX = 4, 8, 2
F32, BF16 = jnp.float32, jnp.bfloat16

score_scale = 168.0 ** (-0.5)


def hop(block, axis, n, step):
    return lax.ppermute(block, axis, [(i, (i + step) % n) for i in range(n)])


def seq_shift(block, distance):
    count = NY * NZ * NX
    route = [(i, i + distance) for i in range(count) if 0 <= i + distance < count]
    return lax.ppermute(block, ("y", "z", "xl"), route)


def ring_gather(block, axis, n, put, buffer, split, between=None):
    me = lax.axis_index(axis)
    half = n // 2
    up = down = block
    steps = []
    for t in range(1, half):
        up, down = hop(up, axis, n, 1), hop(down, axis, n, -1)
        if between is not None:
            up, down = between(t, up, down)
        steps.append((up, down, t))
    top, bottom = hop(split(up, 0), axis, n, 1), hop(split(down, 1), axis, n, -1)
    buffer = put(buffer, block, me, None)
    for up, down, t in steps:
        buffer = put(buffer, up, lax.rem(me + n - t, n), None)
        buffer = put(buffer, down, lax.rem(me + t, n), None)
    far = lax.rem(me + half, n)
    return put(put(buffer, top, far, 0), bottom, far, 1)


def ring_reduce(own, axis, n, split, join, between=None):
    me = lax.axis_index(axis)
    half = n // 2
    far = own(lax.rem(me + half, n))
    up = hop(split(far, 0).astype(BF16), axis, n, 1).astype(F32)
    down = hop(split(far, 1).astype(BF16), axis, n, -1).astype(F32)
    for t in range(2, half + 1):
        ahead = own(lax.rem(me + half - t + 1, n))
        behind = own(lax.rem(me + n - half + t - 1, n))
        if t == 2:
            ahead = join(split(ahead, 0) + up, split(ahead, 1))
            behind = join(split(behind, 0), split(behind, 1) + down)
        else:
            ahead, behind = ahead + up, behind + down
        if between is not None:
            ahead, behind = between(t, ahead, behind)
        up = hop(ahead.astype(BF16), axis, n, 1).astype(F32)
        down = hop(behind.astype(BF16), axis, n, -1).astype(F32)
    return own(me) + up + down


def majors(block, part):
    h = block.shape[0] // 2
    return block[part * h : (part + 1) * h]


def take(array, index, axis):
    return lax.dynamic_index_in_dim(array, index, axis, keepdims=False)


def join_majors(a, b):
    return jnp.concatenate([a, b], 0)


def lanes(block, part):
    h = block.shape[-1] // 2
    return block[..., part * h : (part + 1) * h]


def join_lanes(a, b):
    return jnp.concatenate([a, b], -1)


def put_block(buffer, block, index, part):
    start = (index, 0, 0 if part is None else part * (buffer.shape[-1] // 2))
    return lax.dynamic_update_slice(buffer, block[None], start)


def put_strip(buffer, block, index, part):
    start = (0 if part is None else part * (buffer.shape[0] // 2), index, 0, 0)
    return lax.dynamic_update_slice(buffer, block[:, None], start)


def gather_half(shard, xl):
    other = hop(shard, "xl", NX, 1)
    pair = jnp.where(xl == 0, join_majors(shard, other), join_majors(other, shard))
    rows, width = pair.shape
    blocks = ring_gather(pair, "y", NY, put_block, jnp.zeros((NY, rows, width), BF16), lanes)
    near = jnp.where(xl == 0, blocks[: NY // 2], blocks[NY // 2 :])
    full = jnp.zeros((NY // 2, NZ, rows, width), BF16)


    def rest(near, between):
        return ring_gather(near, "z", NZ, put_strip, full, majors, between).reshape(-1, width)

    return near, rest


def reduce_half(grad, xl, between):
    width = grad.shape[1]
    grad = grad.reshape(NY // 2, NZ, -1, width)
    over_z = ring_reduce(
        lambda i: take(grad, i, 1).astype(F32), "z", NZ, majors, join_majors, between
    )
    none = jnp.zeros_like(over_z)
    blocks = jnp.where(xl == 0, join_majors(over_z, none), join_majors(none, over_z))
    over_y = ring_reduce(lambda i: take(blocks, i, 0), "y", NY, lanes, join_lanes)
    parts = over_y.reshape(NX, -1, width)
    away = hop(take(parts, 1 - xl, 0).astype(BF16), "xl", NX, 1)
    return take(parts, xl, 0) + away.astype(F32)


QB, KB = 256, 128
DOT_ROWS = (((1,), (1,)), ((), ()))
LOG2E = 1.4426950408889634


def attention_kernel(
    q_ref, do_ref, two_ref, one_ref, own_ref, qseg_ref, kseg_ref,
    dq_ref, back_ref, mine_ref, kv, s_buf, dp_buf, ds_buf, acc
):
    tok = q_ref.shape[0]
    hd = q_ref.shape[1] // 2
    span = WIN + QB
    step = pl.program_id(0)

    @pl.when(step == 0)
    def _():
        kv[0:tok] = two_ref[...]
        kv[tok : 2 * tok] = one_ref[...]
        kv[2 * tok :] = own_ref[...]
        acc[...] = jnp.zeros_like(acc)

    base = pl.multiple_of(step * QB, QB)
    q_rows = pl.ds(base, QB)
    q = jnp.concatenate([q_ref[q_rows, :hd], q_ref[q_rows, hd:]], 0)
    do = jnp.concatenate([do_ref[q_rows, :hd], do_ref[q_rows, hd:]], 0)
    qseg = qseg_ref[step]
    r_minus_c = lax.broadcasted_iota(jnp.int32, (KB, QB), 1) - lax.broadcasted_iota(
        jnp.int32, (KB, QB), 0
    )
    chunks = span // KB

    def fold(x, op):
        return op(x.reshape(KB // 8, 8, 2 * QB), axis=0)

    def at(i):
        c = pl.multiple_of(i * KB, KB)
        return c, pl.ds(c, KB), pl.ds(pl.multiple_of(base + c, KB), KB)

    def score(i, peak):
        c, here, rows = at(i)
        s = lax.dot_general(kv[rows, :hd], q, DOT_ROWS, preferred_element_type=F32)
        kseg = kseg_ref[rows, :]
        kseg = jnp.concatenate([kseg] * (QB // kseg.shape[1]), 1)
        ok = (kseg == qseg) & (r_minus_c < c) & (r_minus_c >= c - WIN)
        s = jnp.where(jnp.concatenate([ok, ok], 1), s * (score_scale * LOG2E), -1e30)
        s_buf[here] = s
        dp_buf[here] = lax.dot_general(kv[rows, hd:], do, DOT_ROWS, preferred_element_type=F32)
        return jnp.maximum(peak, fold(s, jnp.max))

    peak = lax.fori_loop(0, chunks, score, jnp.full((8, 2 * QB), -1e30, F32))
    peak = jnp.max(peak, axis=0, keepdims=True)

    def power(i, denom):
        _, here, _ = at(i)
        p = jnp.exp2(s_buf[here] - peak)
        s_buf[here] = p
        return denom + fold(p, jnp.sum)

    denom = lax.fori_loop(0, chunks, power, jnp.zeros((8, 2 * QB), F32))
    inverse = 1.0 / jnp.sum(denom, axis=0, keepdims=True)

    def value(i, delta):
        _, here, rows = at(i)
        p = s_buf[here] * inverse
        s_buf[here] = p
        low = p.astype(BF16)
        acc[rows, hd:] += jnp.dot(low, do, preferred_element_type=F32)
        return delta + fold(low.astype(F32) * dp_buf[here], jnp.sum)

    delta = lax.fori_loop(0, chunks, value, jnp.zeros((8, 2 * QB), F32))
    delta = jnp.sum(delta, axis=0, keepdims=True)

    def key(i, none):
        _, here, rows = at(i)
        ds = (s_buf[here] * (dp_buf[here] - delta)).astype(BF16)
        ds_buf[here] = ds
        acc[rows, :hd] += jnp.dot(ds, q, preferred_element_type=F32)
        return none

    lax.fori_loop(0, chunks, key, 0)
    k_turned = kv[pl.ds(base, span), :hd].T
    dq = jnp.dot(k_turned, ds_buf[...], preferred_element_type=F32) * score_scale
    dq = dq.T.astype(BF16)
    dq_ref[q_rows, :hd] = dq[:QB]
    dq_ref[q_rows, hd:] = dq[QB:]

    @pl.when(step == pl.num_programs(0) - 1)
    def _():
        back_ref[:, :hd] = (acc[: 2 * tok, :hd] * score_scale).astype(BF16)
        back_ref[:, hd:] = acc[: 2 * tok, hd:].astype(BF16)
        mine_ref[:, :hd] = acc[2 * tok :, :hd] * score_scale
        mine_ref[:, hd:] = acc[2 * tok :, hd:]


def attention(q, do, kv_two, kv_one, kv_own, qseg, kseg):
    tok, width = q.shape
    span = WIN + QB
    whole = pl.BlockSpec(memory_space=pltpu.VMEM)
    flops = 10 * (2 * tok) * span * (width // 2)
    return pl.pallas_call(
        attention_kernel,
        grid=(tok // QB,),
        in_specs=[whole] * 7,
        out_specs=[whole] * 3,
        out_shape=[
            jax.ShapeDtypeStruct((tok, width), BF16),
            jax.ShapeDtypeStruct((2 * tok, width), BF16),
            jax.ShapeDtypeStruct((tok, width), F32),
        ],
        scratch_shapes=[
            pltpu.VMEM((3 * tok, width), BF16),
            pltpu.VMEM((span, 2 * QB), F32),
            pltpu.VMEM((span, 2 * QB), F32),
            pltpu.VMEM((span, 2 * QB), BF16),
            pltpu.VMEM((3 * tok, width), F32),
        ],
        compiler_params=pltpu.CompilerParams(vmem_limit_bytes=24 << 20),
        cost_estimate=pl.CostEstimate(
            flops=flops, bytes_accessed=8 << 20, transcendentals=2 * tok * span
        ),
    )(q, do, kv_two, kv_one, kv_own, qseg, kseg)


def weight_grad_kernel(own_ref, par_ref, g_ref, h_ref, o_ref):
    total = jnp.dot(own_ref[...], g_ref[...], preferred_element_type=F32)
    total = total + jnp.dot(par_ref[...], h_ref[...], preferred_element_type=F32)
    o_ref[...] = total.astype(BF16)


def weight_grad(own_turned, par_turned, own_grads, par_grads):
    depth, tok = own_turned.shape
    width = own_grads.shape[1]
    block = depth // 8
    left = pl.BlockSpec((block, tok), lambda i: (i, 0))
    right = pl.BlockSpec((tok, width), lambda i: (0, 0))
    return pl.pallas_call(
        weight_grad_kernel,
        grid=(8,),
        in_specs=[left, left, right, right],
        out_specs=pl.BlockSpec((block, width), lambda i: (i, 0)),
        out_shape=jax.ShapeDtypeStruct((depth, width), BF16),
        compiler_params=pltpu.CompilerParams(vmem_limit_bytes=16 << 20),
        cost_estimate=pl.CostEstimate(
            flops=4 * depth * tok * width, bytes_accessed=12 << 20, transcendentals=0
        ),
    )(own_turned, par_turned, own_grads, par_grads)


def copy_kernel(where, x_ref, o_ref):
    o_ref[...] = x_ref[...]


def piece(inputs, where):
    tok, depth = inputs.shape
    rows, cols = tok // 4, depth // 2
    return pl.pallas_call(
        copy_kernel,
        grid_spec=pltpu.PrefetchScalarGridSpec(
            num_scalar_prefetch=1,
            grid=(2,),
            in_specs=[pl.BlockSpec((rows, cols), lambda i, w: (2 * w[0] + i, w[1]))],
            out_specs=pl.BlockSpec((rows, cols), lambda i, w: (i, 0)),
        ),
        out_shape=jax.ShapeDtypeStruct((2 * rows, cols), inputs.dtype),
        compiler_params=pltpu.CompilerParams(vmem_limit_bytes=8 << 20),
        cost_estimate=pl.CostEstimate(flops=0, bytes_accessed=3 << 20, transcendentals=0),
    )(where, inputs)


def turn_kernel(where, x_ref, o_ref):
    o_ref[...] = x_ref[...].T


def turned(inputs, where, depth):
    tok = inputs.shape[0]
    steps = 7
    cols = depth // steps
    return pl.pallas_call(
        turn_kernel,
        grid_spec=pltpu.PrefetchScalarGridSpec(
            num_scalar_prefetch=1,
            grid=(steps,),
            in_specs=[pl.BlockSpec((tok, cols), lambda i, w: (0, steps * w[0] + i))],
            out_specs=pl.BlockSpec((cols, tok), lambda i, w: (i, 0)),
        ),
        out_shape=jax.ShapeDtypeStruct((depth, tok), inputs.dtype),
        compiler_params=pltpu.CompilerParams(vmem_limit_bytes=8 << 20),
        cost_estimate=pl.CostEstimate(flops=0, bytes_accessed=6 << 20, transcendentals=0),
    )(where, inputs)


def project_kernel(where, x_ref, w_ref, *o_refs):
    step = pl.program_id(0)
    width = o_refs[0].shape[1]
    for g, o_ref in enumerate(o_refs):
        part = jnp.dot(
            x_ref[...], w_ref[:, g * width : (g + 1) * width], preferred_element_type=F32
        )

        @pl.when(step == 0)
        def _():
            o_ref[...] = part

        @pl.when(step > 0)
        def _():
            o_ref[...] += part


def project(inputs, where, weight, groups):
    tok = inputs.shape[0]
    depth, width = weight.shape
    steps = 3
    cols = depth // steps
    out = jax.ShapeDtypeStruct((tok, width // groups), F32)
    return pl.pallas_call(
        project_kernel,
        grid_spec=pltpu.PrefetchScalarGridSpec(
            num_scalar_prefetch=1,
            grid=(steps,),
            in_specs=[
                pl.BlockSpec((tok, cols), lambda i, w: (0, steps * w[0] + i)),
                pl.BlockSpec((cols, width), lambda i, w: (i, 0)),
            ],
            out_specs=[pl.BlockSpec((tok, width // groups), lambda i, w: (0, 0))] * groups,
        ),
        out_shape=[out] * groups,
        compiler_params=pltpu.CompilerParams(vmem_limit_bytes=16 << 20),
        cost_estimate=pl.CostEstimate(
            flops=2 * tok * depth * width, bytes_accessed=8 << 20, transcendentals=0
        ),
    )(where, inputs, weight)


def far_kernel(where, w_ref, g_ref, h_ref, o_ref):
    tok = g_ref.shape[0]
    for i, ref in enumerate((g_ref, h_ref)):
        part = lax.dot_general(w_ref[...], ref[...], DOT_ROWS, preferred_element_type=F32)
        o_ref[:, i * tok : (i + 1) * tok] = part.astype(BF16)


def near_kernel(where, w_ref, g_ref, h_ref, r_ref, own_ref, low_ref):
    tok = g_ref.shape[0]
    for i, ref in enumerate((g_ref, h_ref)):
        part = lax.dot_general(w_ref[...], ref[...], DOT_ROWS, preferred_element_type=F32)
        part = part + r_ref[:, i * tok : (i + 1) * tok].astype(F32)
        low_ref[:, i * tok : (i + 1) * tok] = part.astype(BF16)
        if i == 0:
            own_ref[...] = part


def input_term(where, weight, own_grads, par_grads, received=None):
    depth, width = weight.shape
    tok = own_grads.shape[0]
    steps = 4
    rows = depth // 2 // steps
    grads = pl.BlockSpec((tok, width), lambda i, w: (0, 0))
    both = pl.BlockSpec((rows, 2 * tok), lambda i, w: (i, 0))
    in_specs = [pl.BlockSpec((rows, width), lambda i, w: (steps * w[0] + i, 0)), grads, grads]
    low = jax.ShapeDtypeStruct((depth // 2, 2 * tok), BF16)
    if received is None:
        kernel, out_specs, out_shape, more = far_kernel, both, low, ()
    else:
        kernel, more = near_kernel, (received,)
        in_specs.append(both)
        out_specs = [pl.BlockSpec((rows, tok), lambda i, w: (i, 0)), both]
        out_shape = [jax.ShapeDtypeStruct((depth // 2, tok), F32), low]
    return pl.pallas_call(
        kernel,
        grid_spec=pltpu.PrefetchScalarGridSpec(
            num_scalar_prefetch=1, grid=(steps,), in_specs=in_specs, out_specs=out_specs
        ),
        out_shape=out_shape,
        compiler_params=pltpu.CompilerParams(vmem_limit_bytes=16 << 20),
        cost_estimate=pl.CostEstimate(
            flops=2 * tok * depth * width, bytes_accessed=6 << 20, transcendentals=0
        ),
    )(where, weight, own_grads, par_grads, *more)


def after(value, *others):
    return lax.optimization_barrier((value, *others))[0]


def per_device(inputs, queries, out_grad, segment_ids, k_weight, v_weight, k_gain):
    tok, depth = inputs.shape
    hd = queries.shape[2]
    heads = queries.shape[1]
    groups = k_weight.shape[1] // hd
    seq_index = lax.axis_index(("y", "z", "xl"))
    xl, xh, core = lax.axis_index("xl"), lax.axis_index("xh"), lax.axis_index("c")
    xl_array = jnp.full((1,), xl, jnp.int32)
    zero_array = jnp.zeros((1,), jnp.int32)

    def group(g):
        return slice(2 * g * hd, 2 * (g + 1) * hd)

    shard = jnp.concatenate(
        [w[:, g * hd : (g + 1) * hd] for g in range(groups) for w in (k_weight, v_weight)], 1
    )
    half = depth // 2
    some = hop(piece(inputs, jnp.stack([core, 1 - xl]).astype(jnp.int32)), "xl", NX, 1)
    near, gather_rest = gather_half(shard, xl)
    near, seg = lax.optimization_barrier((near, segment_ids))
    own_turned = turned(inputs, after(xl_array, near), half)
    held = {}

    def meanwhile(t, up, down):
        if t == 2:
            up, down, held["turned"] = lax.optimization_barrier((up, down, own_turned))
        return up, down

    weight = gather_rest(near, meanwhile)
    own_turned = held["turned"]
    rest = hop(some, "c", 2, 1)
    par_in = jnp.where(core == 0, join_majors(some, rest), join_majors(rest, some))

    seg_one, seg_two = seq_shift(seg, 1), seq_shift(seg, 2)
    key_seg = jnp.concatenate(
        [
            jnp.where(seq_index >= 2, seg_two, -1),
            jnp.where(seq_index >= 1, seg_one, -1),
            segment_ids,
        ],
        0,
    )
    key_seg = jnp.broadcast_to(key_seg[:, None], (3 * tok, 128))
    query_seg = segment_ids.reshape(tok // QB, 1, QB)
    q_flat = after(queries, near).reshape(tok, heads * hd)
    do_flat = after(out_grad, near).reshape(tok, heads * hd)

    par_raw = project(par_in, zero_array, weight, groups)
    from_par = [hop(raw, "xl", NX, 1) for raw in par_raw]
    own_raw = project(inputs, after(xl_array, *par_raw), weight, groups)
    par_turned = turned(par_in, after(zero_array, *own_raw), half)
    from_par[0], par_turned = lax.optimization_barrier((from_par[0], par_turned))

    def forward(own_raw, from_par):
        raw = own_raw + from_par
        k_raw = raw[:, :hd]
        k_inv = lax.rsqrt(jnp.mean(k_raw * k_raw, axis=-1, keepdims=True) + 1e-06)
        k_normed = k_raw * k_inv
        own = jnp.concatenate([k_normed * k_gain, raw[:, hd:]], 1).astype(BF16)
        return own, k_normed, k_inv

    def backward(own, k_normed, k_inv, g):
        one, two = seq_shift(own, 1), seq_shift(own, 2)
        dq, back, mine = attention(
            q_flat[:, group(g)], do_flat[:, group(g)], two, one, own, query_seg, key_seg
        )
        grads = (
            mine
            + seq_shift(back[tok:], -1).astype(F32)
            + seq_shift(back[:tok], -2).astype(F32)
        )
        normed_grad = grads[:, :hd] * k_gain
        raw_grad = (
            normed_grad - k_normed * jnp.mean(normed_grad * k_normed, axis=-1, keepdims=True)
        ) * k_inv
        low = jnp.concatenate([raw_grad, grads[:, hd:]], 1).astype(BF16)
        return dq, low, hop(low, "xl", NX, 1)

    state = [forward(own_raw[0], from_par[0])]
    for g in range(1, groups):
        state.append(forward(own_raw[g], after(from_par[g], state[-1][0])))
    dqs, lows, pars = zip(*[backward(*state[g], g) for g in range(groups)])
    own_grads, par_grads = jnp.concatenate(lows, 1), jnp.concatenate(pars, 1)

    keep = xh == xl
    core_array = jnp.full((1,), core, jnp.int32)
    far = input_term(1 - core_array, weight, own_grads, par_grads)
    received = hop(far, "c", 2, 1)

    def between(t, ahead, behind):
        if t == 2:
            own_part, low = input_term(core_array, weight, own_grads, par_grads, received)
            first = jnp.where(keep, low[:, tok:], low[:, :tok])
            held["own"] = own_part
            ahead, behind, held["first"], held["second"] = lax.optimization_barrier(
                (ahead, behind, first, low[:, tok:])
            )
        return ahead, behind

    par_later = after(par_grads, far)
    grad = weight_grad(own_turned, par_turned, own_grads, par_later)
    grad = reduce_half(grad, xl, between)
    cols = [grad[:, i * hd : (i + 1) * hd] for i in range(2 * groups)]
    k_weight_grad = jnp.concatenate(cols[0::2], 1)
    v_weight_grad = jnp.concatenate(cols[1::2], 1)
    query_grad = jnp.concatenate(dqs, 1).reshape(tok, heads, hd)

    first = lax.ppermute(held["first"], ("xl", "xh"), [(0, 2), (3, 1), (1, 0), (2, 3)])
    second = lax.ppermute(held["second"], ("xl", "xh"), [(1, 2), (2, 1)])
    inputs_grad = jnp.where(keep, held["own"], second.astype(F32)) + first.astype(F32)
    return inputs_grad.astype(BF16).T, query_grad, k_weight_grad, v_weight_grad


def solution(mesh):
    fine = Mesh(mesh.devices.reshape(NY, NZ, NX, 2, 2), ("y", "z", "xl", "xh", "c"))
    seq, head = ("y", "z", "xl"), ("xh", "c")
    in_specs = (
        P(seq, None),
        P(seq, head, None),
        P(seq, head, None),
        P(seq),
        P(seq, head),
        P(seq, head),
        P(),
    )
    out_specs = (P(seq, head), P(seq, head, None), P(seq, head), P(seq, head))
    return jax.shard_map(
        per_device, mesh=fine, in_specs=in_specs, out_specs=out_specs, check_vma=False
    )
```

```python
import jax
import jax.numpy as jnp
from jax import lax
from jax.experimental import pallas as pl
from jax.experimental.pallas import tpu as pltpu
from jax.sharding import Mesh, PartitionSpec as P

WIN = 1024
NY, NZ, NX = 4, 8, 2
F32, BF16 = jnp.float32, jnp.bfloat16

score_scale = 168.0 ** (-0.5)


def hop(block, axis, n, step):
    return lax.ppermute(block, axis, [(i, (i + step) % n) for i in range(n)])


def seq_shift(block, distance):
    count = NY * NZ * NX
    route = [(i, i + distance) for i in range(count) if 0 <= i + distance < count]
    return lax.ppermute(block, ("y", "z", "xl"), route)


def ring_gather(block, axis, n, put, buffer, split, between=None):
    me = lax.axis_index(axis)
    half = n // 2
    up = down = block
    steps = []
    for t in range(1, half):
        up, down = hop(up, axis, n, 1), hop(down, axis, n, -1)
        if between is not None:
            up, down = between(t, up, down)
        steps.append((up, down, t))
    top, bottom = hop(split(up, 0), axis, n, 1), hop(split(down, 1), axis, n, -1)
    buffer = put(buffer, block, me, None)
    for up, down, t in steps:
        buffer = put(buffer, up, lax.rem(me + n - t, n), None)
        buffer = put(buffer, down, lax.rem(me + t, n), None)
    far = lax.rem(me + half, n)
    return put(put(buffer, top, far, 0), bottom, far, 1)


def ring_reduce(own, axis, n, split, join, between=None):
    me = lax.axis_index(axis)
    half = n // 2
    far = own(lax.rem(me + half, n))
    up = hop(split(far, 0).astype(BF16), axis, n, 1)
    down = hop(split(far, 1).astype(BF16), axis, n, -1)
    up, down = up.astype(F32), down.astype(F32)
    for t in range(2, half + 1):
        ahead = own(lax.rem(me + half - t + 1, n))
        behind = own(lax.rem(me + n - half + t - 1, n))
        if t == 2:
            ahead = join(split(ahead, 0) + up, split(ahead, 1))
            behind = join(split(behind, 0), split(behind, 1) + down)
        else:
            ahead, behind = ahead + up, behind + down
        if between is not None:
            ahead, behind = between(t, ahead, behind)
        ahead, behind = ahead.astype(BF16), behind.astype(BF16)
        up, down = hop(ahead, axis, n, 1), hop(behind, axis, n, -1)
        up, down = up.astype(F32), down.astype(F32)
    return own(me) + up + down


def majors(block, part):
    h = block.shape[0] // 2
    return block[part * h : (part + 1) * h]


def take(array, index, axis):
    return lax.dynamic_index_in_dim(array, index, axis, keepdims=False)


def join_majors(a, b):
    return jnp.concatenate([a, b], 0)


def lanes(block, part):
    h = block.shape[-1] // 2
    return block[..., part * h : (part + 1) * h]


def join_lanes(a, b):
    return jnp.concatenate([a, b], -1)


def put_block(buffer, block, index, part):
    start = (index, 0, 0 if part is None else part * (buffer.shape[-1] // 2))
    return lax.dynamic_update_slice(buffer, block[None], start)


def put_strip(buffer, block, index, part):
    start = (0 if part is None else part * (buffer.shape[0] // 2), index, 0, 0)
    return lax.dynamic_update_slice(buffer, block[:, None], start)


def gather_half(shard, xl):
    other = hop(shard, "xl", NX, 1)
    pair = jnp.where(xl == 0, join_majors(shard, other), join_majors(other, shard))
    rows, width = pair.shape
    blocks = ring_gather(pair, "y", NY, put_block, jnp.zeros((NY, rows, width), BF16), lanes)
    near = jnp.where(xl == 0, blocks[: NY // 2], blocks[NY // 2 :])
    full = jnp.zeros((NY // 2, NZ, rows, width), BF16)


    def rest(near, between):
        return ring_gather(near, "z", NZ, put_strip, full, majors, between).reshape(-1, width)

    return near, rest


def reduce_half(grad, xl, between):
    width = grad.shape[1]
    grad = grad.reshape(NY // 2, NZ, -1, width)
    over_z = ring_reduce(
        lambda i: take(grad, i, 1).astype(F32), "z", NZ, majors, join_majors, between
    )
    none = jnp.zeros_like(over_z)
    blocks = jnp.where(xl == 0, join_majors(over_z, none), join_majors(none, over_z))
    over_y = ring_reduce(lambda i: take(blocks, i, 0), "y", NY, lanes, join_lanes)
    parts = over_y.reshape(NX, -1, width)
    away = hop(take(parts, 1 - xl, 0).astype(BF16), "xl", NX, 1)
    return take(parts, xl, 0) + away.astype(F32)


QB, KB = 256, 640
SEG_ROWS = 16
DOT_ROWS = (((1,), (1,)), ((), ()))
LOG2E = 1.4426950408889634


def attention_kernel(
    q_ref, do_ref, two_ref, one_ref, own_ref, qseg_ref,
    dq_ref, back_ref, mine_ref, kv, kseg_ref, s_buf, dp_buf, ds_buf, acc
):
    tok = q_ref.shape[0]
    hd = q_ref.shape[1] // 2
    span = WIN + QB
    step = pl.program_id(0)

    @pl.when(step == 0)
    def _():
        for i, ref in enumerate((two_ref, one_ref, own_ref)):
            kv[i * tok : (i + 1) * tok] = ref[:tok]
            ids = ref[tok:].astype(F32).T
            for j in range(tok // ids.shape[0]):
                low = i * tok + j * ids.shape[0]
                column = ids[:, j : j + 1]
                kseg_ref[low : low + ids.shape[0]] = jnp.broadcast_to(column, (ids.shape[0], 128))
        acc[...] = jnp.zeros_like(acc)

    base = pl.multiple_of(step * QB, QB)
    q_rows = pl.ds(base, QB)
    q = jnp.concatenate([q_ref[q_rows, :hd], q_ref[q_rows, hd:]], 0)
    do = jnp.concatenate([do_ref[q_rows, :hd], do_ref[q_rows, hd:]], 0)
    qseg = qseg_ref[step]
    r_minus_c = lax.broadcasted_iota(jnp.int32, (KB, QB), 1) - lax.broadcasted_iota(
        jnp.int32, (KB, QB), 0
    )
    chunks = span // KB

    def fold(x, op):
        return op(x.reshape(KB // 8, 8, 2 * QB), axis=0)

    def at(i):
        c = pl.multiple_of(i * KB, 128)
        return c, pl.ds(c, KB), pl.ds(pl.multiple_of(base + c, 128), KB)

    def score(i, peak):
        c, here, rows = at(i)
        s = lax.dot_general(kv[rows, :hd], q, DOT_ROWS, preferred_element_type=F32)
        kseg = kseg_ref[rows, :]
        kseg = jnp.concatenate([kseg] * (QB // kseg.shape[1]), 1)
        ok = (kseg == qseg) & (r_minus_c < c) & (r_minus_c >= c - WIN)
        s = jnp.where(jnp.concatenate([ok, ok], 1), s * (score_scale * LOG2E), -1e30)
        s_buf[here] = s
        dp_buf[here] = lax.dot_general(kv[rows, hd:], do, DOT_ROWS, preferred_element_type=F32)
        return jnp.maximum(peak, fold(s, jnp.max))

    peak = lax.fori_loop(0, chunks, score, jnp.full((8, 2 * QB), -1e30, F32))
    peak = jnp.max(peak, axis=0, keepdims=True)

    def power(i, denom):
        _, here, _ = at(i)
        p = jnp.exp2(s_buf[here] - peak)
        s_buf[here] = p
        return denom + fold(p, jnp.sum)

    denom = lax.fori_loop(0, chunks, power, jnp.zeros((8, 2 * QB), F32))
    inverse = 1.0 / jnp.sum(denom, axis=0, keepdims=True)

    def value(i, delta):
        _, here, rows = at(i)
        p = s_buf[here] * inverse
        s_buf[here] = p
        low = p.astype(BF16)
        acc[rows, hd:] += jnp.dot(low, do, preferred_element_type=F32)
        return delta + fold(low.astype(F32) * dp_buf[here], jnp.sum)

    delta = lax.fori_loop(0, chunks, value, jnp.zeros((8, 2 * QB), F32))
    delta = jnp.sum(delta, axis=0, keepdims=True)

    def key(i, none):
        _, here, rows = at(i)
        ds = (s_buf[here] * (dp_buf[here] - delta)).astype(BF16)
        ds_buf[here] = ds
        acc[rows, :hd] += jnp.dot(ds, q, preferred_element_type=F32)
        return none

    lax.fori_loop(0, chunks, key, 0)
    k_turned = kv[pl.ds(base, span), :hd].T
    dq = jnp.dot(k_turned, ds_buf[...], preferred_element_type=F32) * score_scale
    dq = dq.T.astype(BF16)
    dq_ref[q_rows, :hd] = dq[:QB]
    dq_ref[q_rows, hd:] = dq[QB:]

    @pl.when(step == pl.num_programs(0) - 1)
    def _():
        back_ref[:, :hd] = (acc[: 2 * tok, :hd] * score_scale).astype(BF16)
        back_ref[:, hd:] = acc[: 2 * tok, hd:].astype(BF16)
        mine_ref[:, :hd] = acc[2 * tok :, :hd] * score_scale
        mine_ref[:, hd:] = acc[2 * tok :, hd:]


def attention(q, do, kv_two, kv_one, kv_own, qseg):
    tok, width = q.shape
    span = WIN + QB
    whole = pl.BlockSpec(memory_space=pltpu.VMEM)
    flops = 10 * (2 * tok) * span * (width // 2)
    return pl.pallas_call(
        attention_kernel,
        grid=(tok // QB,),
        in_specs=[whole] * 6,
        out_specs=[whole] * 3,
        out_shape=[
            jax.ShapeDtypeStruct((tok, width), BF16),
            jax.ShapeDtypeStruct((2 * tok, width), BF16),
            jax.ShapeDtypeStruct((tok, width), F32),
        ],
        scratch_shapes=[
            pltpu.VMEM((3 * tok, width), BF16),
            pltpu.VMEM((3 * tok, 128), F32),
            pltpu.VMEM((span, 2 * QB), F32),
            pltpu.VMEM((span, 2 * QB), F32),
            pltpu.VMEM((span, 2 * QB), BF16),
            pltpu.VMEM((3 * tok, width), F32),
        ],
        compiler_params=pltpu.CompilerParams(vmem_limit_bytes=24 << 20),
        cost_estimate=pl.CostEstimate(
            flops=flops, bytes_accessed=8 << 20, transcendentals=2 * tok * span
        ),
    )(q, do, kv_two, kv_one, kv_own, qseg)


def weight_grad_kernel(own_ref, par_ref, g_ref, h_ref, o_ref):
    total = jnp.dot(own_ref[...], g_ref[...], preferred_element_type=F32)
    total = total + jnp.dot(par_ref[...], h_ref[...], preferred_element_type=F32)
    o_ref[...] = total.astype(BF16)


def weight_grad(own_turned, par_turned, own_grads, par_grads):
    depth, tok = own_turned.shape
    width = own_grads.shape[1]
    block = depth // 8
    left = pl.BlockSpec((block, tok), lambda i: (i, 0))
    right = pl.BlockSpec((tok, width), lambda i: (0, 0))
    return pl.pallas_call(
        weight_grad_kernel,
        grid=(8,),
        in_specs=[left, left, right, right],
        out_specs=pl.BlockSpec((block, width), lambda i: (i, 0)),
        out_shape=jax.ShapeDtypeStruct((depth, width), BF16),
        compiler_params=pltpu.CompilerParams(vmem_limit_bytes=16 << 20),
        cost_estimate=pl.CostEstimate(
            flops=4 * depth * tok * width, bytes_accessed=12 << 20, transcendentals=0
        ),
    )(own_turned, par_turned, own_grads, par_grads)


def copy_kernel(where, x_ref, o_ref):
    o_ref[...] = x_ref[...]


def piece(inputs, where):
    tok, depth = inputs.shape
    rows, cols = tok // 4, depth // 2
    return pl.pallas_call(
        copy_kernel,
        grid_spec=pltpu.PrefetchScalarGridSpec(
            num_scalar_prefetch=1,
            grid=(2,),
            in_specs=[pl.BlockSpec((rows, cols), lambda i, w: (2 * w[0] + i, w[1]))],
            out_specs=pl.BlockSpec((rows, cols), lambda i, w: (i, 0)),
        ),
        out_shape=jax.ShapeDtypeStruct((2 * rows, cols), inputs.dtype),
        compiler_params=pltpu.CompilerParams(vmem_limit_bytes=8 << 20),
        cost_estimate=pl.CostEstimate(flops=0, bytes_accessed=3 << 20, transcendentals=0),
    )(where, inputs)


def turn_kernel(where, x_ref, o_ref):
    o_ref[...] = x_ref[...].T


def turned(inputs, where, depth):
    tok = inputs.shape[0]
    steps = 7
    cols = depth // steps
    return pl.pallas_call(
        turn_kernel,
        grid_spec=pltpu.PrefetchScalarGridSpec(
            num_scalar_prefetch=1,
            grid=(steps,),
            in_specs=[pl.BlockSpec((tok, cols), lambda i, w: (0, steps * w[0] + i))],
            out_specs=pl.BlockSpec((cols, tok), lambda i, w: (i, 0)),
        ),
        out_shape=jax.ShapeDtypeStruct((depth, tok), inputs.dtype),
        compiler_params=pltpu.CompilerParams(vmem_limit_bytes=8 << 20),
        cost_estimate=pl.CostEstimate(flops=0, bytes_accessed=6 << 20, transcendentals=0),
    )(where, inputs)


def project_kernel(where, x_ref, w_ref, *o_refs):
    step = pl.program_id(0)
    width = o_refs[0].shape[1]
    for g, o_ref in enumerate(o_refs):
        part = jnp.dot(
            x_ref[...], w_ref[:, g * width : (g + 1) * width], preferred_element_type=F32
        )

        @pl.when(step == 0)
        def _():
            o_ref[...] = part

        @pl.when(step > 0)
        def _():
            o_ref[...] += part


def project(inputs, where, weight, groups):
    tok = inputs.shape[0]
    depth, width = weight.shape
    steps = 3
    cols = depth // steps
    out = jax.ShapeDtypeStruct((tok, width // groups), F32)
    return pl.pallas_call(
        project_kernel,
        grid_spec=pltpu.PrefetchScalarGridSpec(
            num_scalar_prefetch=1,
            grid=(steps,),
            in_specs=[
                pl.BlockSpec((tok, cols), lambda i, w: (0, steps * w[0] + i)),
                pl.BlockSpec((cols, width), lambda i, w: (i, 0)),
            ],
            out_specs=[pl.BlockSpec((tok, width // groups), lambda i, w: (0, 0))] * groups,
        ),
        out_shape=[out] * groups,
        compiler_params=pltpu.CompilerParams(vmem_limit_bytes=16 << 20),
        cost_estimate=pl.CostEstimate(
            flops=2 * tok * depth * width, bytes_accessed=8 << 20, transcendentals=0
        ),
    )(where, inputs, weight)


def far_kernel(where, w_ref, g_ref, h_ref, o_ref):
    tok = g_ref.shape[0]
    for i, ref in enumerate((g_ref, h_ref)):
        part = lax.dot_general(w_ref[...], ref[...], DOT_ROWS, preferred_element_type=F32)
        o_ref[:, i * tok : (i + 1) * tok] = part.astype(BF16)


def near_kernel(where, w_ref, g_ref, h_ref, r_ref, own_ref, low_ref):
    tok = g_ref.shape[0]
    for i, ref in enumerate((g_ref, h_ref)):
        part = lax.dot_general(w_ref[...], ref[...], DOT_ROWS, preferred_element_type=F32)
        part = part + r_ref[:, i * tok : (i + 1) * tok].astype(F32)
        low_ref[:, i * tok : (i + 1) * tok] = part.astype(BF16)
        if i == 0:
            own_ref[...] = part


def input_term(where, weight, own_grads, par_grads, received=None):
    depth, width = weight.shape
    tok = own_grads.shape[0]
    steps = 4
    rows = depth // 2 // steps
    grads = pl.BlockSpec((tok, width), lambda i, w: (0, 0))
    both = pl.BlockSpec((rows, 2 * tok), lambda i, w: (i, 0))
    in_specs = [pl.BlockSpec((rows, width), lambda i, w: (steps * w[0] + i, 0)), grads, grads]
    low = jax.ShapeDtypeStruct((depth // 2, 2 * tok), BF16)
    if received is None:
        kernel, out_specs, out_shape, more = far_kernel, both, low, ()
    else:
        kernel, more = near_kernel, (received,)
        in_specs.append(both)
        out_specs = [pl.BlockSpec((rows, tok), lambda i, w: (i, 0)), both]
        out_shape = [jax.ShapeDtypeStruct((depth // 2, tok), F32), low]
    return pl.pallas_call(
        kernel,
        grid_spec=pltpu.PrefetchScalarGridSpec(
            num_scalar_prefetch=1, grid=(steps,), in_specs=in_specs, out_specs=out_specs
        ),
        out_shape=out_shape,
        compiler_params=pltpu.CompilerParams(vmem_limit_bytes=16 << 20),
        cost_estimate=pl.CostEstimate(
            flops=2 * tok * depth * width, bytes_accessed=6 << 20, transcendentals=0
        ),
    )(where, weight, own_grads, par_grads, *more)


def after(value, *others):
    return lax.optimization_barrier((value, *others))[0]


def per_device(inputs, queries, out_grad, segment_ids, k_weight, v_weight, k_gain):
    tok, depth = inputs.shape
    hd = queries.shape[2]
    heads = queries.shape[1]
    groups = k_weight.shape[1] // hd
    xl, xh, core = lax.axis_index("xl"), lax.axis_index("xh"), lax.axis_index("c")
    xl_array = jnp.full((1,), xl, jnp.int32)
    zero_array = jnp.zeros((1,), jnp.int32)

    def group(g):
        return slice(2 * g * hd, 2 * (g + 1) * hd)

    shard = jnp.concatenate(
        [w[:, g * hd : (g + 1) * hd] for g in range(groups) for w in (k_weight, v_weight)], 1
    )
    half = depth // 2
    some = hop(piece(inputs, jnp.stack([core, 1 - xl]).astype(jnp.int32)), "xl", NX, 1)
    near, gather_rest = gather_half(shard, xl)
    near, seg = lax.optimization_barrier((near, segment_ids))
    own_turned = turned(inputs, after(xl_array, near), half)
    held = {}

    def meanwhile(t, up, down):
        if t == 2:
            up, down, held["turned"] = lax.optimization_barrier((up, down, own_turned))
        return up, down

    weight = gather_rest(near, meanwhile)
    own_turned = held["turned"]
    rest = hop(some, "c", 2, 1)
    par_in = jnp.where(core == 0, join_majors(some, rest), join_majors(rest, some))

    ids = (seg + 1).astype(F32)
    query_seg = ids.reshape(tok // QB, 1, QB)
    key_seg = jnp.zeros((SEG_ROWS, 2 * hd), BF16)
    key_seg = key_seg.at[: tok // (2 * hd)].set(ids.astype(BF16).reshape(-1, 2 * hd))
    q_flat = after(queries, near).reshape(tok, heads * hd)
    do_flat = after(out_grad, near).reshape(tok, heads * hd)

    par_raw = project(par_in, zero_array, weight, groups)
    from_par = [hop(par_raw[0], "xl", NX, 1)]
    from_par.append(hop(after(par_raw[1], from_par[0]), "xl", NX, 1))
    own_raw = project(inputs, after(xl_array, *par_raw), weight, groups)
    par_turned = turned(par_in, after(zero_array, *own_raw), half)
    from_par[0], par_turned = lax.optimization_barrier((from_par[0], par_turned))

    def forward(own_raw, from_par, gain):
        raw = own_raw + from_par
        k_raw = raw[:, :hd]
        k_inv = lax.rsqrt(jnp.mean(k_raw * k_raw, axis=-1, keepdims=True) + 1e-06)
        k_normed = k_raw * k_inv
        own = jnp.concatenate([k_normed * gain, raw[:, hd:]], 1).astype(BF16)
        return join_majors(own, key_seg), k_normed, k_inv

    def attend(own, g):
        one, two = seq_shift(own, 1), seq_shift(own, 2)
        dq, back, mine = attention(
            q_flat[:, group(g)], do_flat[:, group(g)], two, one, own, query_seg
        )
        one, two = seq_shift(back[tok:], -1), seq_shift(back[:tok], -2)
        return dq, mine, one, two

    def backward(k_normed, k_inv, mine, one, two, gain):
        grads = mine + one.astype(F32) + two.astype(F32)
        normed_grad = grads[:, :hd] * gain
        raw_grad = (
            normed_grad - k_normed * jnp.mean(normed_grad * k_normed, axis=-1, keepdims=True)
        ) * k_inv
        return jnp.concatenate([raw_grad, grads[:, hd:]], 1).astype(BF16)

    state = [forward(own_raw[0], from_par[0], k_gain)]
    for g in range(1, groups):
        arrived, gain = after(from_par[g], state[-1][0]), after(k_gain, state[-1][0])
        state.append(forward(own_raw[g], arrived, gain))
    sent = [attend(state[g][0], g) for g in range(groups)]
    dqs = [t[0] for t in sent]
    lows = []
    for g in range(groups):
        mine, one, two = sent[g][1:]
        if lows:
            mine = after(mine, lows[-1])
        gain = after(k_gain, mine)
        lows.append(backward(*state[g][1:], mine, one, two, gain))
    pars = [hop(low, "xl", NX, 1) for low in lows]
    own_grads, par_grads = jnp.concatenate(lows, 1), jnp.concatenate(pars, 1)

    keep = xh == xl
    core_array = jnp.full((1,), core, jnp.int32)
    far = input_term(1 - core_array, weight, own_grads, par_grads)
    received = hop(far, "c", 2, 1)

    def between(t, ahead, behind):
        if t == 2:
            own_part, low = input_term(core_array, weight, own_grads, par_grads, received)
            first = jnp.where(keep, low[:, tok:], low[:, :tok])
            held["own"] = own_part
            ahead, behind, held["first"], held["second"] = lax.optimization_barrier(
                (ahead, behind, first, low[:, tok:])
            )
        return ahead, behind

    par_later = after(par_grads, far)
    grad = weight_grad(own_turned, par_turned, own_grads, par_later)
    grad = reduce_half(grad, xl, between)
    cols = [grad[:, i * hd : (i + 1) * hd] for i in range(2 * groups)]
    k_weight_grad = jnp.concatenate(cols[0::2], 1)
    v_weight_grad = jnp.concatenate(cols[1::2], 1)
    query_grad = jnp.concatenate(dqs, 1).reshape(tok, heads, hd)

    first = lax.ppermute(held["first"], ("xl", "xh"), [(0, 2), (3, 1), (1, 0), (2, 3)])
    second = lax.ppermute(held["second"], ("xl", "xh"), [(1, 2), (2, 1)])
    inputs_grad = jnp.where(keep, held["own"], second.astype(F32)) + first.astype(F32)
    return inputs_grad.astype(BF16).T, query_grad, k_weight_grad, v_weight_grad


def solution(mesh):
    fine = Mesh(mesh.devices.reshape(NY, NZ, NX, 2, 2), ("y", "z", "xl", "xh", "c"))
    seq, head = ("y", "z", "xl"), ("xh", "c")
    in_specs = (
        P(seq, None),
        P(seq, head, None),
        P(seq, head, None),
        P(seq),
        P(seq, head),
        P(seq, head),
        P(),
    )
    out_specs = (P(seq, head), P(seq, head, None), P(seq, head), P(seq, head))

    return jax.shard_map(
        per_device, mesh=fine, in_specs=in_specs, out_specs=out_specs, check_vma=False
    )
```

```python
import jax
import jax.numpy as jnp
from jax import lax
from jax.experimental import pallas as pl
from jax.experimental.pallas import tpu as pltpu
from jax.sharding import Mesh, PartitionSpec as P

WIN = 1024
NY, NZ, NX = 4, 8, 2
F32, BF16 = jnp.float32, jnp.bfloat16

score_scale = 168.0 ** (-0.5)


def hop(block, axis, n, step):
    return lax.ppermute(block, axis, [(i, (i + step) % n) for i in range(n)])


def seq_shift(block, distance):
    count = NY * NZ * NX
    route = [(i, i + distance) for i in range(count) if 0 <= i + distance < count]
    return lax.ppermute(block, ("y", "z", "xl"), route)


def ring_gather(block, axis, n, put, buffer, split, between=None):
    me = lax.axis_index(axis)
    half = n // 2
    up = down = block
    steps = []
    for t in range(1, half):
        up, down = hop(up, axis, n, 1), hop(down, axis, n, -1)
        if between is not None:
            up, down = between(t, up, down)
        steps.append((up, down, t))
    top, bottom = hop(split(up, 0), axis, n, 1), hop(split(down, 1), axis, n, -1)
    buffer = put(buffer, block, me, None)
    for up, down, t in steps:
        buffer = put(buffer, up, lax.rem(me + n - t, n), None)
        buffer = put(buffer, down, lax.rem(me + t, n), None)
    far = lax.rem(me + half, n)
    return put(put(buffer, top, far, 0), bottom, far, 1)


def ring_reduce(own, axis, n, split, join, between=None):
    me = lax.axis_index(axis)
    half = n // 2
    far = own(lax.rem(me + half, n))
    up = hop(split(far, 0).astype(BF16), axis, n, 1)
    down = hop(split(far, 1).astype(BF16), axis, n, -1)
    up, down = up.astype(F32), down.astype(F32)
    for t in range(2, half + 1):
        ahead = own(lax.rem(me + half - t + 1, n))
        behind = own(lax.rem(me + n - half + t - 1, n))
        if t == 2:
            ahead = join(split(ahead, 0) + up, split(ahead, 1))
            behind = join(split(behind, 0), split(behind, 1) + down)
        else:
            ahead, behind = ahead + up, behind + down
        if between is not None:
            ahead, behind = between(t, ahead, behind)
        ahead, behind = ahead.astype(BF16), behind.astype(BF16)
        up, down = hop(ahead, axis, n, 1), hop(behind, axis, n, -1)
        up, down = up.astype(F32), down.astype(F32)
    return own(me) + up + down


def majors(block, part):
    h = block.shape[0] // 2
    return block[part * h : (part + 1) * h]


def take(array, index, axis):
    return lax.dynamic_index_in_dim(array, index, axis, keepdims=False)


def join_majors(a, b):
    return jnp.concatenate([a, b], 0)


SWAP = [(2 * h + i, 2 * h + 1 - i, h) for h in (0, 1) for i in (0, 1)]
NEAR = [(2 * h + i, 3 - 2 * h - i, h) for h in (0, 1) for i in (0, 1)]
FAR = [(2 * h + i, 2 - 2 * h + i, h) for h in (0, 1) for i in (0, 1)]


def y_route(block, route, back):
    pairs = [(a * NX + xl, b * NX + xl) for a, b, xl in route]
    return lax.ppermute(block, ("y", "xl"), [(b, a) for a, b in pairs] if back else pairs)


def y_place(xl):
    y = lax.axis_index("y")
    return y // 2 == xl, lax.rem(y, 2) == 0


def put_strip(buffer, block, index, part):
    start = (0 if part is None else part * (buffer.shape[0] // 2), index, 0, 0)
    return lax.dynamic_update_slice(buffer, block[:, None], start)


def gather_half(shard, xl):
    other = hop(shard, "xl", NX, 1)
    pair = jnp.where(xl == 0, join_majors(shard, other), join_majors(other, shard))
    rows, width = pair.shape
    holder, even = y_place(xl)
    swap, near, far = [y_route(pair, route, False) for route in (SWAP, NEAR, FAR)]
    one, two = jnp.where(holder, pair, far), jnp.where(holder, swap, near)
    near = jnp.stack([jnp.where(even, one, two), jnp.where(even, two, one)])
    full = jnp.zeros((NY // 2, NZ, rows, width), BF16)


    def rest(near, between):
        return ring_gather(near, "z", NZ, put_strip, full, majors, between).reshape(-1, width)

    return near, rest


def reduce_half(grad, xl, between):
    width = grad.shape[1]
    grad = grad.reshape(NY // 2, NZ, -1, width)
    over_z = ring_reduce(
        lambda i: take(grad, i, 1).astype(F32), "z", NZ, majors, join_majors, between
    )
    holder, even = y_place(xl)
    mine = jnp.where(even, over_z[0], over_z[1])
    other = jnp.where(even, over_z[1], over_z[0]).astype(BF16)
    over_y = jnp.where(holder, mine, 0.0)
    for block, route in ((other, SWAP), (other, NEAR), (mine.astype(BF16), FAR)):
        over_y = over_y + y_route(block, route, True).astype(F32)
    parts = over_y.reshape(NX, -1, width)
    away = hop(take(parts, 1 - xl, 0).astype(BF16), "xl", NX, 1)
    return take(parts, xl, 0) + away.astype(F32)


QB, KB = 256, 256
SEG_ROWS = 16
DOT_ROWS = (((1,), (1,)), ((), ()))
LOG2E = 1.4426950408889634


def attention_kernel(
    q_ref, do_ref, two_ref, one_ref, own_ref, qseg_ref,
    dq_ref, back_ref, mine_ref, kv, kseg_ref, s_buf, dp_buf, ds_buf, acc
):
    tok = q_ref.shape[0]
    hd = q_ref.shape[1] // 2
    span = WIN + QB
    step = pl.program_id(0)

    @pl.when(step == 0)
    def _():
        for i, ref in enumerate((two_ref, one_ref, own_ref)):
            kv[i * tok : (i + 1) * tok] = ref[:tok]
            ids = ref[tok:].astype(F32).T
            for j in range(tok // ids.shape[0]):
                low = i * tok + j * ids.shape[0]
                column = ids[:, j : j + 1]
                kseg_ref[low : low + ids.shape[0]] = jnp.broadcast_to(column, (ids.shape[0], 128))
        acc[...] = jnp.zeros_like(acc)

    base = pl.multiple_of(step * QB, QB)
    q_rows = pl.ds(base, QB)
    q = jnp.concatenate([q_ref[q_rows, :hd], q_ref[q_rows, hd:]], 0)
    do = jnp.concatenate([do_ref[q_rows, :hd], do_ref[q_rows, hd:]], 0)
    qseg = qseg_ref[step]
    r_minus_c = lax.broadcasted_iota(jnp.int32, (KB, QB), 1) - lax.broadcasted_iota(
        jnp.int32, (KB, QB), 0
    )
    chunks = span // KB

    def each(body, carry):
        for i in range(chunks):
            carry = body(i, carry)
        return carry

    def fold(x, op):
        return op(x.reshape(KB // 8, 8, 2 * QB), axis=0)

    def at(i):
        c = i * KB
        return c, pl.ds(c, KB), pl.ds(pl.multiple_of(base + c, 128), KB)

    def score(i, peak):
        c, here, rows = at(i)
        s = lax.dot_general(kv[rows, :hd], q, DOT_ROWS, preferred_element_type=F32)
        kseg = kseg_ref[rows, :]
        kseg = jnp.concatenate([kseg] * (QB // kseg.shape[1]), 1)
        ok = kseg == qseg
        if c < QB:
            ok = ok & (r_minus_c < c)
        if c + KB > WIN:
            ok = ok & (r_minus_c >= c - WIN)
        s = jnp.where(jnp.concatenate([ok, ok], 1), s * (score_scale * LOG2E), -1e30)
        s_buf[here] = s
        dp_buf[here] = lax.dot_general(kv[rows, hd:], do, DOT_ROWS, preferred_element_type=F32)
        return jnp.maximum(peak, fold(s, jnp.max))

    peak = each(score, jnp.full((8, 2 * QB), -1e30, F32))
    peak = jnp.max(peak, axis=0, keepdims=True)

    def power(i, denom):
        _, here, _ = at(i)
        p = jnp.exp2(s_buf[here] - peak)
        s_buf[here] = p
        return denom + fold(p, jnp.sum)

    denom = each(power, jnp.zeros((8, 2 * QB), F32))
    inverse = 1.0 / jnp.sum(denom, axis=0, keepdims=True)

    def value(i, delta):
        _, here, rows = at(i)
        p = s_buf[here] * inverse
        s_buf[here] = p
        low = p.astype(BF16)
        acc[rows, hd:] += jnp.dot(low, do, preferred_element_type=F32)
        return delta + fold(low.astype(F32) * dp_buf[here], jnp.sum)

    delta = each(value, jnp.zeros((8, 2 * QB), F32))
    delta = jnp.sum(delta, axis=0, keepdims=True)

    def key(i, none):
        _, here, rows = at(i)
        ds = (s_buf[here] * (dp_buf[here] - delta)).astype(BF16)
        ds_buf[here] = ds
        acc[rows, :hd] += jnp.dot(ds, q, preferred_element_type=F32)
        return none

    each(key, 0)
    k_turned = kv[pl.ds(base, span), :hd].T
    dq = jnp.dot(k_turned, ds_buf[...], preferred_element_type=F32) * score_scale
    dq = dq.T.astype(BF16)
    dq_ref[q_rows, :hd] = dq[:QB]
    dq_ref[q_rows, hd:] = dq[QB:]

    @pl.when(step == pl.num_programs(0) - 1)
    def _():
        back_ref[:, :hd] = (acc[: 2 * tok, :hd] * score_scale).astype(BF16)
        back_ref[:, hd:] = acc[: 2 * tok, hd:].astype(BF16)
        mine_ref[:, :hd] = acc[2 * tok :, :hd] * score_scale
        mine_ref[:, hd:] = acc[2 * tok :, hd:]


def attention(q, do, kv_two, kv_one, kv_own, qseg):
    tok, width = q.shape
    span = WIN + QB
    whole = pl.BlockSpec(memory_space=pltpu.VMEM)
    flops = 10 * (2 * tok) * span * (width // 2)
    return pl.pallas_call(
        attention_kernel,
        grid=(tok // QB,),
        in_specs=[whole] * 6,
        out_specs=[whole] * 3,
        out_shape=[
            jax.ShapeDtypeStruct((tok, width), BF16),
            jax.ShapeDtypeStruct((2 * tok, width), BF16),
            jax.ShapeDtypeStruct((tok, width), F32),
        ],
        scratch_shapes=[
            pltpu.VMEM((3 * tok, width), BF16),
            pltpu.VMEM((3 * tok, 128), F32),
            pltpu.VMEM((span, 2 * QB), F32),
            pltpu.VMEM((span, 2 * QB), F32),
            pltpu.VMEM((span, 2 * QB), BF16),
            pltpu.VMEM((3 * tok, width), F32),
        ],
        compiler_params=pltpu.CompilerParams(vmem_limit_bytes=24 << 20),
        cost_estimate=pl.CostEstimate(
            flops=flops, bytes_accessed=8 << 20, transcendentals=2 * tok * span
        ),
    )(q, do, kv_two, kv_one, kv_own, qseg)


def weight_grad_kernel(own_ref, par_ref, g_ref, h_ref, o_ref):
    total = jnp.dot(own_ref[...], g_ref[...], preferred_element_type=F32)
    total = total + jnp.dot(par_ref[...], h_ref[...], preferred_element_type=F32)
    o_ref[...] = total.astype(BF16)


def weight_grad(own_turned, par_turned, own_grads, par_grads):
    depth, tok = own_turned.shape
    width = own_grads.shape[1]
    block = depth // 8
    left = pl.BlockSpec((block, tok), lambda i: (i, 0))
    right = pl.BlockSpec((tok, width), lambda i: (0, 0))
    return pl.pallas_call(
        weight_grad_kernel,
        grid=(8,),
        in_specs=[left, left, right, right],
        out_specs=pl.BlockSpec((block, width), lambda i: (i, 0)),
        out_shape=jax.ShapeDtypeStruct((depth, width), BF16),
        compiler_params=pltpu.CompilerParams(vmem_limit_bytes=60 << 20),
        cost_estimate=pl.CostEstimate(
            flops=4 * depth * tok * width, bytes_accessed=12 << 20, transcendentals=0
        ),
    )(own_turned, par_turned, own_grads, par_grads)


def copy_kernel(where, x_ref, o_ref):
    o_ref[...] = x_ref[...]


def piece(inputs, where):
    tok, depth = inputs.shape
    rows, cols = tok // 4, depth // 2
    return pl.pallas_call(
        copy_kernel,
        grid_spec=pltpu.PrefetchScalarGridSpec(
            num_scalar_prefetch=1,
            grid=(2,),
            in_specs=[pl.BlockSpec((rows, cols), lambda i, w: (2 * w[0] + i, w[1]))],
            out_specs=pl.BlockSpec((rows, cols), lambda i, w: (i, 0)),
        ),
        out_shape=jax.ShapeDtypeStruct((2 * rows, cols), inputs.dtype),
        compiler_params=pltpu.CompilerParams(vmem_limit_bytes=60 << 20),
        cost_estimate=pl.CostEstimate(flops=0, bytes_accessed=3 << 20, transcendentals=0),
    )(where, inputs)


def turn_kernel(where, x_ref, o_ref):
    o_ref[...] = x_ref[...].T


def turned(inputs, where, depth):
    tok = inputs.shape[0]
    steps = 7
    cols = depth // steps
    return pl.pallas_call(
        turn_kernel,
        grid_spec=pltpu.PrefetchScalarGridSpec(
            num_scalar_prefetch=1,
            grid=(steps,),
            in_specs=[pl.BlockSpec((tok, cols), lambda i, w: (0, steps * w[0] + i))],
            out_specs=pl.BlockSpec((cols, tok), lambda i, w: (i, 0)),
        ),
        out_shape=jax.ShapeDtypeStruct((depth, tok), inputs.dtype),
        compiler_params=pltpu.CompilerParams(vmem_limit_bytes=60 << 20),
        cost_estimate=pl.CostEstimate(flops=0, bytes_accessed=6 << 20, transcendentals=0),
    )(where, inputs)


def project_kernel(where, x_ref, w_ref, *o_refs):
    step = pl.program_id(1)
    width = o_refs[0].shape[1]
    for g, o_ref in enumerate(o_refs):
        part = jnp.dot(
            x_ref[...], w_ref[:, g * width : (g + 1) * width], preferred_element_type=F32
        )

        @pl.when(step == 0)
        def _():
            o_ref[...] = part

        @pl.when(step > 0)
        def _():
            o_ref[...] += part


def project(inputs, where, weight, groups):
    tok = inputs.shape[0]
    depth, width = weight.shape
    steps = 3
    cols, rows = depth // steps, tok // 2
    out = jax.ShapeDtypeStruct((tok, width // groups), F32)
    return pl.pallas_call(
        project_kernel,
        grid_spec=pltpu.PrefetchScalarGridSpec(
            num_scalar_prefetch=1,
            grid=(2, steps),
            in_specs=[
                pl.BlockSpec((rows, cols), lambda j, i, w: (j, steps * w[0] + i)),
                pl.BlockSpec((cols, width), lambda j, i, w: (i, 0)),
            ],
            out_specs=[pl.BlockSpec((rows, width // groups), lambda j, i, w: (j, 0))] * groups,
        ),
        out_shape=[out] * groups,
        compiler_params=pltpu.CompilerParams(vmem_limit_bytes=16 << 20),
        cost_estimate=pl.CostEstimate(
            flops=2 * tok * depth * width, bytes_accessed=8 << 20, transcendentals=0
        ),
    )(where, inputs, weight)


def far_kernel(where, w_ref, g_ref, h_ref, o_ref):
    tok = g_ref.shape[0]
    for i, ref in enumerate((g_ref, h_ref)):
        part = lax.dot_general(w_ref[...], ref[...], DOT_ROWS, preferred_element_type=F32)
        o_ref[:, i * tok : (i + 1) * tok] = part.astype(BF16)


def near_kernel(where, w_ref, g_ref, h_ref, r_ref, own_ref, low_ref):
    tok = g_ref.shape[0]
    for i, ref in enumerate((g_ref, h_ref)):
        part = lax.dot_general(w_ref[...], ref[...], DOT_ROWS, preferred_element_type=F32)
        part = part + r_ref[:, i * tok : (i + 1) * tok].astype(F32)
        low_ref[:, i * tok : (i + 1) * tok] = part.astype(BF16)
        if i == 0:
            own_ref[...] = part


def input_term(where, weight, own_grads, par_grads, received=None):
    depth, width = weight.shape
    tok = own_grads.shape[0]
    steps = 4
    rows = depth // 2 // steps
    grads = pl.BlockSpec((tok, width), lambda i, w: (0, 0))
    both = pl.BlockSpec((rows, 2 * tok), lambda i, w: (i, 0))
    in_specs = [pl.BlockSpec((rows, width), lambda i, w: (steps * w[0] + i, 0)), grads, grads]
    low = jax.ShapeDtypeStruct((depth // 2, 2 * tok), BF16)
    if received is None:
        kernel, out_specs, out_shape, more = far_kernel, both, low, ()
    else:
        kernel, more = near_kernel, (received,)
        in_specs.append(both)
        out_specs = [pl.BlockSpec((rows, tok), lambda i, w: (i, 0)), both]
        out_shape = [jax.ShapeDtypeStruct((depth // 2, tok), F32), low]
    return pl.pallas_call(
        kernel,
        grid_spec=pltpu.PrefetchScalarGridSpec(
            num_scalar_prefetch=1, grid=(steps,), in_specs=in_specs, out_specs=out_specs
        ),
        out_shape=out_shape,
        compiler_params=pltpu.CompilerParams(vmem_limit_bytes=16 << 20),
        cost_estimate=pl.CostEstimate(
            flops=2 * tok * depth * width, bytes_accessed=6 << 20, transcendentals=0
        ),
    )(where, weight, own_grads, par_grads, *more)


def after(value, *others):
    return lax.optimization_barrier((value, *others))[0]


def per_device(inputs, queries, out_grad, segment_ids, k_weight, v_weight, k_gain):
    tok, depth = inputs.shape
    hd = queries.shape[2]
    heads = queries.shape[1]
    groups = k_weight.shape[1] // hd
    xl, xh, core = lax.axis_index("xl"), lax.axis_index("xh"), lax.axis_index("c")
    xl_array = jnp.full((1,), xl, jnp.int32)
    zero_array = jnp.zeros((1,), jnp.int32)

    def group(g):
        return slice(2 * g * hd, 2 * (g + 1) * hd)

    shard = jnp.concatenate(
        [w[:, g * hd : (g + 1) * hd] for g in range(groups) for w in (k_weight, v_weight)], 1
    )
    half = depth // 2
    some = hop(piece(inputs, jnp.stack([core, 1 - xl]).astype(jnp.int32)), "xl", NX, 1)
    near, gather_rest = gather_half(shard, xl)
    near, seg = lax.optimization_barrier((near, segment_ids))
    own_turned = turned(inputs, after(xl_array, near), half)
    held = {}

    def meanwhile(t, up, down):
        if t == 2:
            up, down, held["turned"] = lax.optimization_barrier((up, down, own_turned))
        return up, down

    weight = gather_rest(near, meanwhile)
    own_turned = held["turned"]
    rest = hop(some, "c", 2, 1)
    par_in = jnp.where(core == 0, join_majors(some, rest), join_majors(rest, some))

    ids = (seg + 1).astype(F32)
    query_seg = ids.reshape(tok // QB, 1, QB)
    key_seg = jnp.zeros((SEG_ROWS, 2 * hd), BF16)
    key_seg = key_seg.at[: tok // (2 * hd)].set(ids.astype(BF16).reshape(-1, 2 * hd))
    q_flat = after(queries, near).reshape(tok, heads * hd)
    do_flat = after(out_grad, near).reshape(tok, heads * hd)

    par_raw = project(par_in, zero_array, weight, groups)
    from_par = [hop(par_raw[0], "xl", NX, 1)]
    from_par.append(hop(after(par_raw[1], from_par[0]), "xl", NX, 1))
    own_raw = project(inputs, after(xl_array, *par_raw), weight, groups)
    par_turned = turned(par_in, after(zero_array, *own_raw), half)
    from_par[0], par_turned = lax.optimization_barrier((from_par[0], par_turned))

    def forward(own_raw, from_par, gain):
        raw = own_raw + from_par
        k_raw = raw[:, :hd]
        k_inv = lax.rsqrt(jnp.mean(k_raw * k_raw, axis=-1, keepdims=True) + 1e-06)
        k_normed = k_raw * k_inv
        own = jnp.concatenate([k_normed * gain, raw[:, hd:]], 1).astype(BF16)
        return join_majors(own, key_seg), k_normed, k_inv

    def attend(own, g):
        one, two = seq_shift(own, 1), seq_shift(own, 2)
        dq, back, mine = attention(
            q_flat[:, group(g)], do_flat[:, group(g)], two, one, own, query_seg
        )
        one, two = seq_shift(back[tok:], -1), seq_shift(back[:tok], -2)
        return dq, mine, one, two

    def backward(k_normed, k_inv, mine, one, two, gain):
        grads = mine + one.astype(F32) + two.astype(F32)
        normed_grad = grads[:, :hd] * gain
        raw_grad = (
            normed_grad - k_normed * jnp.mean(normed_grad * k_normed, axis=-1, keepdims=True)
        ) * k_inv
        return jnp.concatenate([raw_grad, grads[:, hd:]], 1).astype(BF16)

    state = [forward(own_raw[0], from_par[0], k_gain)]
    for g in range(1, groups):
        arrived, gain = after(from_par[g], state[-1][0]), after(k_gain, state[-1][0])
        state.append(forward(own_raw[g], arrived, gain))
    sent = [attend(state[g][0], g) for g in range(groups)]
    dqs = [t[0] for t in sent]
    lows = []
    for g in range(groups):
        mine, one, two = sent[g][1:]
        if lows:
            mine = after(mine, lows[-1])
        gain = after(k_gain, mine)
        lows.append(backward(*state[g][1:], mine, one, two, gain))
    pars = [hop(low, "xl", NX, 1) for low in lows]
    own_grads, par_grads = jnp.concatenate(lows, 1), jnp.concatenate(pars, 1)

    keep = xh == xl
    core_array = jnp.full((1,), core, jnp.int32)
    far = input_term(1 - core_array, weight, own_grads, par_grads)
    received = hop(far, "c", 2, 1)

    def between(t, ahead, behind):
        if t == 2:
            own_part, low = input_term(core_array, weight, own_grads, par_grads, received)
            first = jnp.where(keep, low[:, tok:], low[:, :tok])
            held["own"] = own_part
            ahead, behind, held["first"], held["second"] = lax.optimization_barrier(
                (ahead, behind, first, low[:, tok:])
            )
        return ahead, behind

    par_later = after(par_grads, far)
    grad = weight_grad(own_turned, par_turned, own_grads, par_later)
    grad = reduce_half(grad, xl, between)
    cols = [grad[:, i * hd : (i + 1) * hd] for i in range(2 * groups)]
    k_weight_grad = jnp.concatenate(cols[0::2], 1)
    v_weight_grad = jnp.concatenate(cols[1::2], 1)
    query_grad = jnp.concatenate(dqs, 1).reshape(tok, heads, hd)

    first = lax.ppermute(held["first"], ("xl", "xh"), [(0, 2), (3, 1), (1, 0), (2, 3)])
    second = lax.ppermute(held["second"], ("xl", "xh"), [(1, 2), (2, 1)])
    inputs_grad = jnp.where(keep, held["own"], second.astype(F32)) + first.astype(F32)
    return inputs_grad.astype(BF16).T, query_grad, k_weight_grad, v_weight_grad


def solution(mesh):
    fine = Mesh(mesh.devices.reshape(NY, NZ, NX, 2, 2), ("y", "z", "xl", "xh", "c"))
    seq, head = ("y", "z", "xl"), ("xh", "c")
    in_specs = (
        P(seq, None),
        P(seq, head, None),
        P(seq, head, None),
        P(seq),
        P(seq, head),
        P(seq, head),
        P(),
    )
    out_specs = (P(seq, head), P(seq, head, None), P(seq, head), P(seq, head))

    return jax.shard_map(
        per_device, mesh=fine, in_specs=in_specs, out_specs=out_specs, check_vma=False
    )
```

```python
import jax
import jax.numpy as jnp
from jax import lax
from jax.experimental import pallas as pl
from jax.experimental.pallas import tpu as pltpu
from jax.sharding import Mesh, PartitionSpec as P

WIN = 1024
NY, NZ, NX = 4, 8, 2
F32, BF16 = jnp.float32, jnp.bfloat16

score_scale = 168.0 ** (-0.5)


def hop(block, axis, n, step):
    return lax.ppermute(block, axis, [(i, (i + step) % n) for i in range(n)])


def seq_shift(block, distance):
    count = NY * NZ * NX
    route = [(i, i + distance) for i in range(count) if 0 <= i + distance < count]
    return lax.ppermute(block, ("y", "z", "xl"), route)


def ring_gather(block, axis, n, put, buffer, split, between=None):
    me = lax.axis_index(axis)
    half = n // 2
    up = down = block
    steps = []
    for t in range(1, half):
        up, down = hop(up, axis, n, 1), hop(down, axis, n, -1)
        if between is not None:
            up, down = between(t, up, down)
        steps.append((up, down, t))
    top, bottom = hop(split(up, 0), axis, n, 1), hop(split(down, 1), axis, n, -1)
    buffer = put(buffer, block, me, None)
    for up, down, t in steps:
        buffer = put(buffer, up, lax.rem(me + n - t, n), None)
        buffer = put(buffer, down, lax.rem(me + t, n), None)
    far = lax.rem(me + half, n)
    return put(put(buffer, top, far, 0), bottom, far, 1)


def ring_reduce(own, axis, n, split, join, between=None):
    me = lax.axis_index(axis)
    half = n // 2
    far = own(lax.rem(me + half, n))
    up = hop(split(far, 0).astype(BF16), axis, n, 1)
    down = hop(split(far, 1).astype(BF16), axis, n, -1)
    up, down = up.astype(F32), down.astype(F32)
    for t in range(2, half + 1):
        ahead = own(lax.rem(me + half - t + 1, n))
        behind = own(lax.rem(me + n - half + t - 1, n))
        if t == 2:
            ahead = join(split(ahead, 0) + up, split(ahead, 1))
            behind = join(split(behind, 0), split(behind, 1) + down)
        else:
            ahead, behind = ahead + up, behind + down
        if between is not None:
            ahead, behind = between(t, ahead, behind)
        ahead, behind = ahead.astype(BF16), behind.astype(BF16)
        up, down = hop(ahead, axis, n, 1), hop(behind, axis, n, -1)
        up, down = up.astype(F32), down.astype(F32)
    return own(me) + up + down


def majors(block, part):
    h = block.shape[0] // 2
    return block[part * h : (part + 1) * h]


def take(array, index, axis):
    return lax.dynamic_index_in_dim(array, index, axis, keepdims=False)


def join_majors(a, b):
    return jnp.concatenate([a, b], 0)


SWAP = [(2 * h + i, 2 * h + 1 - i, h) for h in (0, 1) for i in (0, 1)]
NEAR = [(2 * h + i, 3 - 2 * h - i, h) for h in (0, 1) for i in (0, 1)]
FAR = [(2 * h + i, 2 - 2 * h + i, h) for h in (0, 1) for i in (0, 1)]


def y_route(block, route, back):
    pairs = [(a * NX + xl, b * NX + xl) for a, b, xl in route]
    return lax.ppermute(block, ("y", "xl"), [(b, a) for a, b in pairs] if back else pairs)


def y_place(xl):
    y = lax.axis_index("y")
    return y // 2 == xl, lax.rem(y, 2) == 0


def put_strip(buffer, block, index, part):
    start = (0 if part is None else part * (buffer.shape[0] // 2), index, 0, 0)
    return lax.dynamic_update_slice(buffer, block[:, None], start)


def gather_half(shard, xl):
    other = hop(shard, "xl", NX, 1)
    pair = jnp.where(xl == 0, join_majors(shard, other), join_majors(other, shard))
    rows, width = pair.shape
    holder, even = y_place(xl)
    swap, near, far = [y_route(pair, route, False) for route in (SWAP, NEAR, FAR)]
    one, two = jnp.where(holder, pair, far), jnp.where(holder, swap, near)
    near = jnp.stack([jnp.where(even, one, two), jnp.where(even, two, one)])
    full = jnp.zeros((NY // 2, NZ, rows, width), BF16)


    def rest(near, between):
        return ring_gather(near, "z", NZ, put_strip, full, majors, between).reshape(-1, width)

    return near, rest


def reduce_half(grad, xl, between):
    width = grad.shape[1]
    grad = grad.reshape(NY // 2, NZ, -1, width)
    over_z = ring_reduce(
        lambda i: take(grad, i, 1).astype(F32), "z", NZ, majors, join_majors, between
    )
    holder, even = y_place(xl)
    mine = jnp.where(even, over_z[0], over_z[1])
    other = jnp.where(even, over_z[1], over_z[0]).astype(BF16)
    over_y = jnp.where(holder, mine, 0.0)
    for block, route in ((other, SWAP), (other, NEAR), (mine.astype(BF16), FAR)):
        over_y = over_y + y_route(block, route, True).astype(F32)
    parts = over_y.reshape(NX, -1, width)
    give = take(parts, 1 - xl, 0).astype(BF16)
    away = hop(give, "xl", NX, 1)
    return take(parts, xl, 0) + away.astype(F32)


QB, KB = 256, 256
SEG_ROWS = 16
DOT_ROWS = (((1,), (1,)), ((), ()))
LOG2E = 1.4426950408889634


def attention_kernel(
    q_ref, do_ref, two_ref, one_ref, own_ref, qseg_ref,
    dq_ref, back_ref, mine_ref, kv, kseg_ref, s_buf, dp_buf, ds_buf, acc
):
    tok = q_ref.shape[0]
    hd = q_ref.shape[1] // 2
    span = WIN + QB
    step = pl.program_id(0)

    @pl.when(step == 0)
    def _():
        for i, ref in enumerate((two_ref, one_ref, own_ref)):
            kv[i * tok : (i + 1) * tok] = ref[:tok]
            ids = ref[tok:].astype(F32).T
            for j in range(tok // ids.shape[0]):
                low = i * tok + j * ids.shape[0]
                column = ids[:, j : j + 1]
                kseg_ref[low : low + ids.shape[0]] = jnp.broadcast_to(column, (ids.shape[0], 128))
        acc[...] = jnp.zeros_like(acc)

    base = pl.multiple_of(step * QB, QB)
    q_rows = pl.ds(base, QB)
    q = jnp.concatenate([q_ref[q_rows, :hd], q_ref[q_rows, hd:]], 0)
    do = jnp.concatenate([do_ref[q_rows, :hd], do_ref[q_rows, hd:]], 0)
    qseg = qseg_ref[step]
    r_minus_c = lax.broadcasted_iota(jnp.int32, (KB, QB), 1) - lax.broadcasted_iota(
        jnp.int32, (KB, QB), 0
    )
    chunks = span // KB

    def each(body, carry):
        for i in range(chunks):
            carry = body(i, carry)
        return carry

    def fold(x, op):
        return op(x.reshape(KB // 8, 8, 2 * QB), axis=0)

    def at(i):
        c = i * KB
        return c, pl.ds(c, KB), pl.ds(pl.multiple_of(base + c, 128), KB)

    def score(i, peak):
        c, here, rows = at(i)
        s = lax.dot_general(kv[rows, :hd], q, DOT_ROWS, preferred_element_type=F32)
        kseg = kseg_ref[rows, :]
        kseg = jnp.concatenate([kseg] * (QB // kseg.shape[1]), 1)
        ok = kseg == qseg
        if c < QB:
            ok = ok & (r_minus_c < c)
        if c + KB > WIN:
            ok = ok & (r_minus_c >= c - WIN)
        s = jnp.where(jnp.concatenate([ok, ok], 1), s * (score_scale * LOG2E), -1e30)
        s_buf[here] = s
        dp_buf[here] = lax.dot_general(kv[rows, hd:], do, DOT_ROWS, preferred_element_type=F32)
        return jnp.maximum(peak, fold(s, jnp.max))

    peak = each(score, jnp.full((8, 2 * QB), -1e30, F32))
    peak = jnp.max(peak, axis=0, keepdims=True)

    def power(i, denom):
        _, here, _ = at(i)
        p = jnp.exp2(s_buf[here] - peak)
        s_buf[here] = p
        return denom + fold(p, jnp.sum)

    denom = each(power, jnp.zeros((8, 2 * QB), F32))
    inverse = 1.0 / jnp.sum(denom, axis=0, keepdims=True)

    def value(i, delta):
        _, here, rows = at(i)
        p = s_buf[here] * inverse
        s_buf[here] = p
        low = p.astype(BF16)
        acc[rows, hd:] += jnp.dot(low, do, preferred_element_type=F32)
        return delta + fold(low.astype(F32) * dp_buf[here], jnp.sum)

    delta = each(value, jnp.zeros((8, 2 * QB), F32))
    delta = jnp.sum(delta, axis=0, keepdims=True)

    def key(i, none):
        _, here, rows = at(i)
        ds = (s_buf[here] * (dp_buf[here] - delta)).astype(BF16)
        ds_buf[here] = ds
        acc[rows, :hd] += jnp.dot(ds, q, preferred_element_type=F32)
        return none

    each(key, 0)
    k_turned = kv[pl.ds(base, span), :hd].T
    dq = jnp.dot(k_turned, ds_buf[...], preferred_element_type=F32) * score_scale
    dq = dq.T.astype(BF16)
    dq_ref[q_rows, :hd] = dq[:QB]
    dq_ref[q_rows, hd:] = dq[QB:]

    @pl.when(step == pl.num_programs(0) - 1)
    def _():
        back_ref[:, :hd] = (acc[: 2 * tok, :hd] * score_scale).astype(BF16)
        back_ref[:, hd:] = acc[: 2 * tok, hd:].astype(BF16)
        mine_ref[:, :hd] = acc[2 * tok :, :hd] * score_scale
        mine_ref[:, hd:] = acc[2 * tok :, hd:]


def attention(q, do, kv_two, kv_one, kv_own, qseg):
    tok, width = q.shape
    span = WIN + QB
    whole = pl.BlockSpec(memory_space=pltpu.VMEM)
    flops = 10 * (2 * tok) * span * (width // 2)
    return pl.pallas_call(
        attention_kernel,
        grid=(tok // QB,),
        in_specs=[whole] * 6,
        out_specs=[whole] * 3,
        out_shape=[
            jax.ShapeDtypeStruct((tok, width), BF16),
            jax.ShapeDtypeStruct((2 * tok, width), BF16),
            jax.ShapeDtypeStruct((tok, width), F32),
        ],
        scratch_shapes=[
            pltpu.VMEM((3 * tok, width), BF16),
            pltpu.VMEM((3 * tok, 128), F32),
            pltpu.VMEM((span, 2 * QB), F32),
            pltpu.VMEM((span, 2 * QB), F32),
            pltpu.VMEM((span, 2 * QB), BF16),
            pltpu.VMEM((3 * tok, width), F32),
        ],
        compiler_params=pltpu.CompilerParams(vmem_limit_bytes=24 << 20),
        cost_estimate=pl.CostEstimate(
            flops=flops, bytes_accessed=8 << 20, transcendentals=2 * tok * span
        ),
    )(q, do, kv_two, kv_one, kv_own, qseg)


def weight_grad_kernel(own_ref, par_ref, g_ref, h_ref, o_ref):
    total = jnp.dot(own_ref[...], g_ref[...], preferred_element_type=F32)
    total = total + jnp.dot(par_ref[...], h_ref[...], preferred_element_type=F32)
    o_ref[...] = total.astype(BF16)


def weight_grad(own_turned, par_turned, own_grads, par_grads):
    depth, tok = own_turned.shape
    width = own_grads.shape[1]
    block = depth // 8
    left = pl.BlockSpec((block, tok), lambda i: (i, 0))
    right = pl.BlockSpec((tok, width), lambda i: (0, 0))
    return pl.pallas_call(
        weight_grad_kernel,
        grid=(8,),
        in_specs=[left, left, right, right],
        out_specs=pl.BlockSpec((block, width), lambda i: (i, 0)),
        out_shape=jax.ShapeDtypeStruct((depth, width), BF16),
        compiler_params=pltpu.CompilerParams(vmem_limit_bytes=16 << 20),
        cost_estimate=pl.CostEstimate(
            flops=4 * depth * tok * width, bytes_accessed=12 << 20, transcendentals=0
        ),
    )(own_turned, par_turned, own_grads, par_grads)


def copy_kernel(where, x_ref, o_ref):
    o_ref[...] = x_ref[...]


def piece(inputs, where):
    tok, depth = inputs.shape
    rows, cols = tok // 4, depth // 2
    return pl.pallas_call(
        copy_kernel,
        grid_spec=pltpu.PrefetchScalarGridSpec(
            num_scalar_prefetch=1,
            grid=(2,),
            in_specs=[pl.BlockSpec((rows, cols), lambda i, w: (2 * w[0] + i, w[1]))],
            out_specs=pl.BlockSpec((rows, cols), lambda i, w: (i, 0)),
        ),
        out_shape=jax.ShapeDtypeStruct((2 * rows, cols), inputs.dtype),
        compiler_params=pltpu.CompilerParams(vmem_limit_bytes=8 << 20),
        cost_estimate=pl.CostEstimate(flops=0, bytes_accessed=3 << 20, transcendentals=0),
    )(where, inputs)


def turn_kernel(where, x_ref, o_ref):
    o_ref[...] = x_ref[...].T


def turned(inputs, where, depth):
    tok = inputs.shape[0]
    steps = 7
    cols = depth // steps
    return pl.pallas_call(
        turn_kernel,
        grid_spec=pltpu.PrefetchScalarGridSpec(
            num_scalar_prefetch=1,
            grid=(steps,),
            in_specs=[pl.BlockSpec((tok, cols), lambda i, w: (0, steps * w[0] + i))],
            out_specs=pl.BlockSpec((cols, tok), lambda i, w: (i, 0)),
        ),
        out_shape=jax.ShapeDtypeStruct((depth, tok), inputs.dtype),
        compiler_params=pltpu.CompilerParams(vmem_limit_bytes=8 << 20),
        cost_estimate=pl.CostEstimate(flops=0, bytes_accessed=6 << 20, transcendentals=0),
    )(where, inputs)


def project_kernel(where, x_ref, w_ref, *o_refs):
    step = pl.program_id(1)
    width = o_refs[0].shape[1]
    for g, o_ref in enumerate(o_refs):
        part = jnp.dot(
            x_ref[...], w_ref[:, g * width : (g + 1) * width], preferred_element_type=F32
        )

        @pl.when(step == 0)
        def _():
            o_ref[...] = part

        @pl.when(step > 0)
        def _():
            o_ref[...] += part


def project(inputs, where, weight, groups):
    tok = inputs.shape[0]
    depth, width = weight.shape
    steps = 3
    cols, rows = depth // steps, tok // 2
    out = jax.ShapeDtypeStruct((tok, width // groups), F32)
    return pl.pallas_call(
        project_kernel,
        grid_spec=pltpu.PrefetchScalarGridSpec(
            num_scalar_prefetch=1,
            grid=(2, steps),
            in_specs=[
                pl.BlockSpec((rows, cols), lambda j, i, w: (j, steps * w[0] + i)),
                pl.BlockSpec((cols, width), lambda j, i, w: (i, 0)),
            ],
            out_specs=[pl.BlockSpec((rows, width // groups), lambda j, i, w: (j, 0))] * groups,
        ),
        out_shape=[out] * groups,
        compiler_params=pltpu.CompilerParams(vmem_limit_bytes=16 << 20),
        cost_estimate=pl.CostEstimate(
            flops=2 * tok * depth * width, bytes_accessed=8 << 20, transcendentals=0
        ),
    )(where, inputs, weight)


def far_kernel(where, w_ref, g_ref, h_ref, o_ref):
    tok = g_ref.shape[0]
    for i, ref in enumerate((g_ref, h_ref)):
        part = lax.dot_general(w_ref[...], ref[...], DOT_ROWS, preferred_element_type=F32)
        o_ref[:, i * tok : (i + 1) * tok] = part.astype(BF16)


def near_kernel(where, w_ref, g_ref, h_ref, r_ref, own_ref, low_ref):
    tok = g_ref.shape[0]
    for i, ref in enumerate((g_ref, h_ref)):
        part = lax.dot_general(w_ref[...], ref[...], DOT_ROWS, preferred_element_type=F32)
        part = part + r_ref[:, i * tok : (i + 1) * tok].astype(F32)
        low_ref[:, i * tok : (i + 1) * tok] = part.astype(BF16)
        if i == 0:
            own_ref[...] = part


def input_term(where, weight, own_grads, par_grads, received=None):
    depth, width = weight.shape
    tok = own_grads.shape[0]
    steps = 4
    rows = depth // 2 // steps
    grads = pl.BlockSpec((tok, width), lambda i, w: (0, 0))
    both = pl.BlockSpec((rows, 2 * tok), lambda i, w: (i, 0))
    in_specs = [pl.BlockSpec((rows, width), lambda i, w: (steps * w[0] + i, 0)), grads, grads]
    low = jax.ShapeDtypeStruct((depth // 2, 2 * tok), BF16)
    if received is None:
        kernel, out_specs, out_shape, more = far_kernel, both, low, ()
    else:
        kernel, more = near_kernel, (received,)
        in_specs.append(both)
        out_specs = [pl.BlockSpec((rows, tok), lambda i, w: (i, 0)), both]
        out_shape = [jax.ShapeDtypeStruct((depth // 2, tok), F32), low]
    return pl.pallas_call(
        kernel,
        grid_spec=pltpu.PrefetchScalarGridSpec(
            num_scalar_prefetch=1, grid=(steps,), in_specs=in_specs, out_specs=out_specs
        ),
        out_shape=out_shape,
        compiler_params=pltpu.CompilerParams(vmem_limit_bytes=16 << 20),
        cost_estimate=pl.CostEstimate(
            flops=2 * tok * depth * width, bytes_accessed=6 << 20, transcendentals=0
        ),
    )(where, weight, own_grads, par_grads, *more)


def finish_kernel(keep, own_ref, first_ref, second_ref, o_ref):
    base = jnp.where(keep[0] == 1, own_ref[...], second_ref[...].astype(F32))
    o_ref[...] = (base + first_ref[...].astype(F32)).astype(BF16)


def finish(keep, own, first, second):
    depth, tok = own.shape
    steps = 4
    block = pl.BlockSpec((depth // steps, tok), lambda i, w: (i, 0))
    return pl.pallas_call(
        finish_kernel,
        grid_spec=pltpu.PrefetchScalarGridSpec(
            num_scalar_prefetch=1, grid=(steps,), in_specs=[block] * 3, out_specs=block
        ),
        out_shape=jax.ShapeDtypeStruct((depth, tok), BF16),
        compiler_params=pltpu.CompilerParams(vmem_limit_bytes=8 << 20),
        cost_estimate=pl.CostEstimate(
            flops=4 * depth * tok, bytes_accessed=10 * depth * tok, transcendentals=0
        ),
    )(keep, own, first, second)


def after(value, *others):
    return lax.optimization_barrier((value, *others))[0]


def per_device(inputs, queries, out_grad, segment_ids, k_weight, v_weight, k_gain):
    tok, depth = inputs.shape
    hd = queries.shape[2]
    heads = queries.shape[1]
    groups = k_weight.shape[1] // hd
    xl, xh, core = lax.axis_index("xl"), lax.axis_index("xh"), lax.axis_index("c")
    xl_array = jnp.full((1,), xl, jnp.int32)
    zero_array = jnp.zeros((1,), jnp.int32)

    def group(g):
        return slice(2 * g * hd, 2 * (g + 1) * hd)

    shard = jnp.concatenate(
        [w[:, g * hd : (g + 1) * hd] for g in range(groups) for w in (k_weight, v_weight)], 1
    )
    half = depth // 2
    some = hop(piece(inputs, jnp.stack([core, 1 - xl]).astype(jnp.int32)), "xl", NX, 1)
    near, gather_rest = gather_half(shard, xl)
    near, seg = lax.optimization_barrier((near, segment_ids))
    own_turned = turned(inputs, after(xl_array, near), half)
    held = {}

    def meanwhile(t, up, down):
        if t == 2:
            up, down, held["turned"] = lax.optimization_barrier((up, down, own_turned))
        return up, down

    weight = gather_rest(near, meanwhile)
    own_turned = held["turned"]
    rest = hop(some, "c", 2, 1)
    par_in = jnp.where(core == 0, join_majors(some, rest), join_majors(rest, some))

    ids = (seg + 1).astype(F32)
    query_seg = ids.reshape(tok // QB, 1, QB)
    key_seg = jnp.zeros((SEG_ROWS, 2 * hd), BF16)
    key_seg = key_seg.at[: tok // (2 * hd)].set(ids.astype(BF16).reshape(-1, 2 * hd))
    q_flat = after(queries, near).reshape(tok, heads * hd)
    do_flat = after(out_grad, near).reshape(tok, heads * hd)

    par_raw = project(par_in, zero_array, weight, groups)
    from_par = [hop(par_raw[0], "xl", NX, 1)]
    from_par.append(hop(after(par_raw[1], from_par[0]), "xl", NX, 1))
    own_raw = project(inputs, after(xl_array, *par_raw), weight, groups)
    par_turned = turned(par_in, after(zero_array, *own_raw), half)
    from_par[0], par_turned = lax.optimization_barrier((from_par[0], par_turned))

    def forward(own_raw, from_par, gain):
        raw = own_raw + from_par
        k_raw = raw[:, :hd]
        k_inv = lax.rsqrt(jnp.mean(k_raw * k_raw, axis=-1, keepdims=True) + 1e-06)
        k_normed = k_raw * k_inv
        own = jnp.concatenate([k_normed * gain, raw[:, hd:]], 1).astype(BF16)
        return join_majors(own, key_seg), k_normed, k_inv

    def attend(own, g):
        one, two = seq_shift(own, 1), seq_shift(own, 2)
        dq, back, mine = attention(
            q_flat[:, group(g)], do_flat[:, group(g)], two, one, own, query_seg
        )
        one, two = seq_shift(back[tok:], -1), seq_shift(back[:tok], -2)
        return dq, mine, one, two

    def backward(k_normed, k_inv, mine, one, two, gain):
        grads = mine + one.astype(F32) + two.astype(F32)
        normed_grad = grads[:, :hd] * gain
        raw_grad = (
            normed_grad - k_normed * jnp.mean(normed_grad * k_normed, axis=-1, keepdims=True)
        ) * k_inv
        return jnp.concatenate([raw_grad, grads[:, hd:]], 1).astype(BF16)

    state = [forward(own_raw[0], from_par[0], k_gain)]
    for g in range(1, groups):
        arrived, gain = after(from_par[g], state[-1][0]), after(k_gain, state[-1][0])
        state.append(forward(own_raw[g], arrived, gain))
    sent = [attend(state[g][0], g) for g in range(groups)]
    dqs = [t[0] for t in sent]
    lows = []
    for g in range(groups):
        mine, one, two = sent[g][1:]
        if lows:
            mine = after(mine, lows[-1])
        gain = after(k_gain, mine)
        lows.append(backward(*state[g][1:], mine, one, two, gain))
    pars = [hop(low, "xl", NX, 1) for low in lows]
    own_grads, par_grads = jnp.concatenate(lows, 1), jnp.concatenate(pars, 1)

    keep = xh == xl
    core_array = jnp.full((1,), core, jnp.int32)
    far = input_term(1 - core_array, weight, own_grads, par_grads)
    received = hop(far, "c", 2, 1)

    def between(t, ahead, behind):
        if t == 2:
            own_part, low = input_term(core_array, weight, own_grads, par_grads, received)
            first = jnp.where(keep, low[:, tok:], low[:, :tok])
            held["own"] = own_part
            ahead, behind, held["first"], held["second"] = lax.optimization_barrier(
                (ahead, behind, first, low[:, tok:])
            )
        return ahead, behind

    par_later = after(par_grads, far)
    grad = weight_grad(own_turned, par_turned, own_grads, par_later)
    grad = reduce_half(grad, xl, between)
    cols = [grad[:, i * hd : (i + 1) * hd] for i in range(2 * groups)]
    k_weight_grad = jnp.concatenate(cols[0::2], 1)
    v_weight_grad = jnp.concatenate(cols[1::2], 1)
    query_grad = jnp.concatenate(dqs, 1).reshape(tok, heads, hd)

    first = lax.ppermute(held["first"], ("xl", "xh"), [(0, 2), (3, 1), (1, 0), (2, 3)])
    second = lax.ppermute(held["second"], ("xl", "xh"), [(1, 2), (2, 1)])
    keep_array = jnp.full((1,), keep, jnp.int32)
    inputs_grad = finish(keep_array, held["own"], first, second)
    return inputs_grad.T, query_grad, k_weight_grad, v_weight_grad


def solution(mesh):
    fine = Mesh(mesh.devices.reshape(NY, NZ, NX, 2, 2), ("y", "z", "xl", "xh", "c"))
    seq, head = ("y", "z", "xl"), ("xh", "c")
    in_specs = (
        P(seq, None),
        P(seq, head, None),
        P(seq, head, None),
        P(seq),
        P(seq, head),
        P(seq, head),
        P(),
    )
    out_specs = (P(seq, head), P(seq, head, None), P(seq, head), P(seq, head))

    return jax.shard_map(
        per_device, mesh=fine, in_specs=in_specs, out_specs=out_specs, check_vma=False
    )
```

```python
import jax
import jax.numpy as jnp
from jax import lax
from jax.experimental import pallas as pl
from jax.experimental.pallas import tpu as pltpu
from jax.sharding import Mesh, PartitionSpec as P

WIN = 1024
NY, NZ, NX = 4, 8, 2
F32, BF16 = jnp.float32, jnp.bfloat16

score_scale = 168.0 ** (-0.5)


def hop(block, axis, n, step):
    return lax.ppermute(block, axis, [(i, (i + step) % n) for i in range(n)])


def seq_shift(block, distance):
    count = NY * NZ * NX
    route = [(i, i + distance) for i in range(count) if 0 <= i + distance < count]
    return lax.ppermute(block, ("y", "z", "xl"), route)


def ring_gather(block, axis, n, put, buffer, split, between=None):
    me = lax.axis_index(axis)
    half = n // 2
    up = down = block
    steps = []
    for t in range(1, half):
        up, down = hop(up, axis, n, 1), hop(down, axis, n, -1)
        if between is not None:
            up, down = between(t, up, down)
        steps.append((up, down, t))
    top, bottom = hop(split(up, 0), axis, n, 1), hop(split(down, 1), axis, n, -1)
    buffer = put(buffer, block, me, None)
    for up, down, t in steps:
        buffer = put(buffer, up, lax.rem(me + n - t, n), None)
        buffer = put(buffer, down, lax.rem(me + t, n), None)
    far = lax.rem(me + half, n)
    return put(put(buffer, top, far, 0), bottom, far, 1)


def ring_reduce(own, axis, n, split, join, between=None):
    me = lax.axis_index(axis)
    half = n // 2
    far = own(lax.rem(me + half, n))
    up = hop(split(far, 0).astype(BF16), axis, n, 1)
    down = hop(split(far, 1).astype(BF16), axis, n, -1)
    up, down = up.astype(F32), down.astype(F32)
    for t in range(2, half + 1):
        ahead = own(lax.rem(me + half - t + 1, n))
        behind = own(lax.rem(me + n - half + t - 1, n))
        if t == 2:
            ahead = join(split(ahead, 0) + up, split(ahead, 1))
            behind = join(split(behind, 0), split(behind, 1) + down)
        else:
            ahead, behind = ahead + up, behind + down
        if between is not None:
            ahead, behind = between(t, ahead, behind)
        ahead, behind = ahead.astype(BF16), behind.astype(BF16)
        up, down = hop(ahead, axis, n, 1), hop(behind, axis, n, -1)
        up, down = up.astype(F32), down.astype(F32)
    return own(me) + up + down


def majors(block, part):
    h = block.shape[0] // 2
    return block[part * h : (part + 1) * h]


def take(array, index, axis):
    return lax.dynamic_index_in_dim(array, index, axis, keepdims=False)


def join_majors(a, b):
    return jnp.concatenate([a, b], 0)


SWAP = [(2 * h + i, 2 * h + 1 - i, h) for h in (0, 1) for i in (0, 1)]
NEAR = [(2 * h + i, 3 - 2 * h - i, h) for h in (0, 1) for i in (0, 1)]
FAR = [(2 * h + i, 2 - 2 * h + i, h) for h in (0, 1) for i in (0, 1)]


def y_route(block, route, back):
    pairs = [(a * NX + xl, b * NX + xl) for a, b, xl in route]
    return lax.ppermute(block, ("y", "xl"), [(b, a) for a, b in pairs] if back else pairs)


def y_place(xl):
    y = lax.axis_index("y")
    return y // 2 == xl, lax.rem(y, 2) == 0


def put_strip(buffer, block, index, part):
    start = (0 if part is None else part * (buffer.shape[0] // 2), index, 0, 0)
    return lax.dynamic_update_slice(buffer, block[:, None], start)


def gather_half(shard, xl):
    other = hop(shard, "xl", NX, 1)
    pair = jnp.where(xl == 0, join_majors(shard, other), join_majors(other, shard))
    rows, width = pair.shape
    holder, even = y_place(xl)
    swap, near, far = [y_route(pair, route, False) for route in (SWAP, NEAR, FAR)]
    one, two = jnp.where(holder, pair, far), jnp.where(holder, swap, near)
    near = jnp.stack([jnp.where(even, one, two), jnp.where(even, two, one)])
    full = jnp.zeros((NY // 2, NZ, rows, width), BF16)


    def rest(near, between):
        return ring_gather(near, "z", NZ, put_strip, full, majors, between).reshape(-1, width)

    return near, rest


def reduce_half(grad, xl, between):
    width = grad.shape[1]
    grad = grad.reshape(NY // 2, NZ, -1, width)
    over_z = ring_reduce(
        lambda i: take(grad, i, 1).astype(F32), "z", NZ, majors, join_majors, between
    )
    holder, even = y_place(xl)
    mine = jnp.where(even, over_z[0], over_z[1])
    other = jnp.where(even, over_z[1], over_z[0]).astype(BF16)
    over_y = jnp.where(holder, mine, 0.0)
    for block, route in ((other, SWAP), (other, NEAR), (mine.astype(BF16), FAR)):
        over_y = over_y + y_route(block, route, True).astype(F32)
    parts = over_y.reshape(NX, -1, width)
    give = take(parts, 1 - xl, 0).astype(BF16)
    away = hop(give, "xl", NX, 1)
    return take(parts, xl, 0) + away.astype(F32)


QB, KB = 256, 256
SEG_ROWS = 16
DOT_ROWS = (((1,), (1,)), ((), ()))
LOG2E = 1.4426950408889634


def attention_kernel(
    q_ref, do_ref, two_ref, one_ref, own_ref, qseg_ref,
    dq_ref, back_ref, mine_ref, kv, kseg_ref, s_buf, dp_buf, ds_buf, acc
):
    tok = q_ref.shape[0]
    hd = q_ref.shape[1] // 2
    span = WIN + QB
    step = pl.program_id(0)

    @pl.when(step == 0)
    def _():
        for i, ref in enumerate((two_ref, one_ref, own_ref)):
            kv[i * tok : (i + 1) * tok] = ref[:tok]
            ids = ref[tok:].astype(F32).T
            for j in range(tok // ids.shape[0]):
                low = i * tok + j * ids.shape[0]
                column = ids[:, j : j + 1]
                kseg_ref[low : low + ids.shape[0]] = jnp.broadcast_to(column, (ids.shape[0], 128))
        acc[...] = jnp.zeros_like(acc)

    base = pl.multiple_of(step * QB, QB)
    q_rows = pl.ds(base, QB)
    q = jnp.concatenate([q_ref[q_rows, :hd], q_ref[q_rows, hd:]], 0)
    do = jnp.concatenate([do_ref[q_rows, :hd], do_ref[q_rows, hd:]], 0)
    qseg = qseg_ref[step]
    r_minus_c = lax.broadcasted_iota(jnp.int32, (KB, QB), 1) - lax.broadcasted_iota(
        jnp.int32, (KB, QB), 0
    )
    chunks = span // KB

    def each(body, carry):
        for i in range(chunks):
            carry = body(i, carry)
        return carry

    def fold(x, op):
        return op(x.reshape(KB // 8, 8, 2 * QB), axis=0)

    def at(i):
        c = i * KB
        return c, pl.ds(c, KB), pl.ds(pl.multiple_of(base + c, 128), KB)

    def score(i, peak):
        c, here, rows = at(i)
        s = lax.dot_general(kv[rows, :hd], q, DOT_ROWS, preferred_element_type=F32)
        kseg = kseg_ref[rows, :]
        kseg = jnp.concatenate([kseg] * (QB // kseg.shape[1]), 1)
        ok = kseg == qseg
        if c < QB:
            ok = ok & (r_minus_c < c)
        if c + KB > WIN:
            ok = ok & (r_minus_c >= c - WIN)
        s = jnp.where(jnp.concatenate([ok, ok], 1), s * (score_scale * LOG2E), -1e30)
        s_buf[here] = s
        dp_buf[here] = lax.dot_general(kv[rows, hd:], do, DOT_ROWS, preferred_element_type=F32)
        return jnp.maximum(peak, fold(s, jnp.max))

    peak = each(score, jnp.full((8, 2 * QB), -1e30, F32))
    peak = jnp.max(peak, axis=0, keepdims=True)

    def power(i, denom):
        _, here, _ = at(i)
        p = jnp.exp2(s_buf[here] - peak)
        s_buf[here] = p
        return denom + fold(p, jnp.sum)

    denom = each(power, jnp.zeros((8, 2 * QB), F32))
    inverse = 1.0 / jnp.sum(denom, axis=0, keepdims=True)

    def value(i, delta):
        _, here, rows = at(i)
        p = s_buf[here] * inverse
        s_buf[here] = p
        low = p.astype(BF16)
        acc[rows, hd:] += jnp.dot(low, do, preferred_element_type=F32)
        return delta + fold(low.astype(F32) * dp_buf[here], jnp.sum)

    delta = each(value, jnp.zeros((8, 2 * QB), F32))
    delta = jnp.sum(delta, axis=0, keepdims=True)

    def key(i, none):
        _, here, rows = at(i)
        ds = (s_buf[here] * (dp_buf[here] - delta)).astype(BF16)
        ds_buf[here] = ds
        acc[rows, :hd] += jnp.dot(ds, q, preferred_element_type=F32)
        return none

    each(key, 0)
    k_turned = kv[pl.ds(base, span), :hd].T
    dq = jnp.dot(k_turned, ds_buf[...], preferred_element_type=F32) * score_scale
    dq = dq.T.astype(BF16)
    dq_ref[q_rows, :hd] = dq[:QB]
    dq_ref[q_rows, hd:] = dq[QB:]

    @pl.when(step == pl.num_programs(0) - 1)
    def _():
        back_ref[:, :hd] = (acc[: 2 * tok, :hd] * score_scale).astype(BF16)
        back_ref[:, hd:] = acc[: 2 * tok, hd:].astype(BF16)
        mine_ref[:, :hd] = acc[2 * tok :, :hd] * score_scale
        mine_ref[:, hd:] = acc[2 * tok :, hd:]


def attention(q, do, kv_two, kv_one, kv_own, qseg):
    tok, width = q.shape
    span = WIN + QB
    whole = pl.BlockSpec(memory_space=pltpu.VMEM)
    flops = 10 * (2 * tok) * span * (width // 2)
    return pl.pallas_call(
        attention_kernel,
        grid=(tok // QB,),
        in_specs=[whole] * 6,
        out_specs=[whole] * 3,
        out_shape=[
            jax.ShapeDtypeStruct((tok, width), BF16),
            jax.ShapeDtypeStruct((2 * tok, width), BF16),
            jax.ShapeDtypeStruct((tok, width), F32),
        ],
        scratch_shapes=[
            pltpu.VMEM((3 * tok, width), BF16),
            pltpu.VMEM((3 * tok, 128), F32),
            pltpu.VMEM((span, 2 * QB), F32),
            pltpu.VMEM((span, 2 * QB), F32),
            pltpu.VMEM((span, 2 * QB), BF16),
            pltpu.VMEM((3 * tok, width), F32),
        ],
        compiler_params=pltpu.CompilerParams(vmem_limit_bytes=24 << 20),
        cost_estimate=pl.CostEstimate(
            flops=flops, bytes_accessed=8 << 20, transcendentals=2 * tok * span
        ),
    )(q, do, kv_two, kv_one, kv_own, qseg)


def weight_grad_kernel(own_ref, par_ref, g_ref, h_ref, o_ref):
    total = jnp.dot(own_ref[...], g_ref[...], preferred_element_type=F32)
    total = total + jnp.dot(par_ref[...], h_ref[...], preferred_element_type=F32)
    o_ref[...] = total.astype(BF16)


def weight_grad(own_turned, par_turned, own_grads, par_grads):
    depth, tok = own_turned.shape
    width = own_grads.shape[1]
    block = depth // 8
    left = pl.BlockSpec((block, tok), lambda i: (i, 0))
    right = pl.BlockSpec((tok, width), lambda i: (0, 0))
    return pl.pallas_call(
        weight_grad_kernel,
        grid=(8,),
        in_specs=[left, left, right, right],
        out_specs=pl.BlockSpec((block, width), lambda i: (i, 0)),
        out_shape=jax.ShapeDtypeStruct((depth, width), BF16),
        compiler_params=pltpu.CompilerParams(vmem_limit_bytes=16 << 20),
        cost_estimate=pl.CostEstimate(
            flops=4 * depth * tok * width, bytes_accessed=12 << 20, transcendentals=0
        ),
    )(own_turned, par_turned, own_grads, par_grads)


def copy_kernel(where, x_ref, o_ref):
    o_ref[...] = x_ref[...]


def piece(inputs, where):
    tok, depth = inputs.shape
    rows, cols = tok // 4, depth // 2
    return pl.pallas_call(
        copy_kernel,
        grid_spec=pltpu.PrefetchScalarGridSpec(
            num_scalar_prefetch=1,
            grid=(2,),
            in_specs=[pl.BlockSpec((rows, cols), lambda i, w: (2 * w[0] + i, w[1]))],
            out_specs=pl.BlockSpec((rows, cols), lambda i, w: (i, 0)),
        ),
        out_shape=jax.ShapeDtypeStruct((2 * rows, cols), inputs.dtype),
        compiler_params=pltpu.CompilerParams(vmem_limit_bytes=8 << 20),
        cost_estimate=pl.CostEstimate(flops=0, bytes_accessed=3 << 20, transcendentals=0),
    )(where, inputs)


def turn_kernel(where, x_ref, o_ref):
    o_ref[...] = x_ref[...].T


def turned(inputs, where, depth):
    tok = inputs.shape[0]
    steps = 7
    cols = depth // steps
    return pl.pallas_call(
        turn_kernel,
        grid_spec=pltpu.PrefetchScalarGridSpec(
            num_scalar_prefetch=1,
            grid=(steps,),
            in_specs=[pl.BlockSpec((tok, cols), lambda i, w: (0, steps * w[0] + i))],
            out_specs=pl.BlockSpec((cols, tok), lambda i, w: (i, 0)),
        ),
        out_shape=jax.ShapeDtypeStruct((depth, tok), inputs.dtype),
        compiler_params=pltpu.CompilerParams(vmem_limit_bytes=8 << 20),
        cost_estimate=pl.CostEstimate(flops=0, bytes_accessed=6 << 20, transcendentals=0),
    )(where, inputs)


def project_kernel(where, x_ref, w_ref, *o_refs):
    step = pl.program_id(1)
    width = o_refs[0].shape[1]
    for g, o_ref in enumerate(o_refs):
        part = jnp.dot(
            x_ref[...], w_ref[:, g * width : (g + 1) * width], preferred_element_type=F32
        )

        @pl.when(step == 0)
        def _():
            o_ref[...] = part

        @pl.when(step > 0)
        def _():
            o_ref[...] += part


def project(inputs, where, weight, groups):
    tok = inputs.shape[0]
    depth, width = weight.shape
    steps = 3
    cols, rows = depth // steps, tok // 2
    out = jax.ShapeDtypeStruct((tok, width // groups), F32)
    return pl.pallas_call(
        project_kernel,
        grid_spec=pltpu.PrefetchScalarGridSpec(
            num_scalar_prefetch=1,
            grid=(2, steps),
            in_specs=[
                pl.BlockSpec((rows, cols), lambda j, i, w: (j, steps * w[0] + i)),
                pl.BlockSpec((cols, width), lambda j, i, w: (i, 0)),
            ],
            out_specs=[pl.BlockSpec((rows, width // groups), lambda j, i, w: (j, 0))] * groups,
        ),
        out_shape=[out] * groups,
        compiler_params=pltpu.CompilerParams(vmem_limit_bytes=16 << 20),
        cost_estimate=pl.CostEstimate(
            flops=2 * tok * depth * width, bytes_accessed=8 << 20, transcendentals=0
        ),
    )(where, inputs, weight)


def far_kernel(where, w_ref, g_ref, h_ref, o_ref):
    tok = g_ref.shape[0]
    for i, ref in enumerate((g_ref, h_ref)):
        part = lax.dot_general(w_ref[...], ref[...], DOT_ROWS, preferred_element_type=F32)
        o_ref[:, i * tok : (i + 1) * tok] = part.astype(BF16)


def near_kernel(where, w_ref, g_ref, h_ref, r_ref, own_ref, low_ref):
    tok = g_ref.shape[0]
    for i, ref in enumerate((g_ref, h_ref)):
        part = lax.dot_general(w_ref[...], ref[...], DOT_ROWS, preferred_element_type=F32)
        part = part + r_ref[:, i * tok : (i + 1) * tok].astype(F32)
        low_ref[:, i * tok : (i + 1) * tok] = part.astype(BF16)
        if i == 0:
            own_ref[...] = part


def input_term(where, weight, own_grads, par_grads, received=None):
    depth, width = weight.shape
    tok = own_grads.shape[0]
    steps = 4
    rows = depth // 2 // steps
    grads = pl.BlockSpec((tok, width), lambda i, w: (0, 0))
    both = pl.BlockSpec((rows, 2 * tok), lambda i, w: (i, 0))
    in_specs = [pl.BlockSpec((rows, width), lambda i, w: (steps * w[0] + i, 0)), grads, grads]
    low = jax.ShapeDtypeStruct((depth // 2, 2 * tok), BF16)
    if received is None:
        kernel, out_specs, out_shape, more = far_kernel, both, low, ()
    else:
        kernel, more = near_kernel, (received,)
        in_specs.append(both)
        out_specs = [pl.BlockSpec((rows, tok), lambda i, w: (i, 0)), both]
        out_shape = [jax.ShapeDtypeStruct((depth // 2, tok), F32), low]
    return pl.pallas_call(
        kernel,
        grid_spec=pltpu.PrefetchScalarGridSpec(
            num_scalar_prefetch=1, grid=(steps,), in_specs=in_specs, out_specs=out_specs
        ),
        out_shape=out_shape,
        compiler_params=pltpu.CompilerParams(vmem_limit_bytes=16 << 20),
        cost_estimate=pl.CostEstimate(
            flops=2 * tok * depth * width, bytes_accessed=6 << 20, transcendentals=0
        ),
    )(where, weight, own_grads, par_grads, *more)


def finish_kernel(keep, own_ref, first_ref, second_ref, o_ref):
    base = jnp.where(keep[0] == 1, own_ref[...], second_ref[...].astype(F32))
    o_ref[...] = (base + first_ref[...].astype(F32)).astype(BF16)


def finish(keep, own, first, second):
    depth, tok = own.shape
    steps = 4
    block = pl.BlockSpec((depth // steps, tok), lambda i, w: (i, 0))
    return pl.pallas_call(
        finish_kernel,
        grid_spec=pltpu.PrefetchScalarGridSpec(
            num_scalar_prefetch=1, grid=(steps,), in_specs=[block] * 3, out_specs=block
        ),
        out_shape=jax.ShapeDtypeStruct((depth, tok), BF16),
        compiler_params=pltpu.CompilerParams(vmem_limit_bytes=8 << 20),
        cost_estimate=pl.CostEstimate(
            flops=4 * depth * tok, bytes_accessed=10 * depth * tok, transcendentals=0
        ),
    )(keep, own, first, second)


def after(value, *others):
    return lax.optimization_barrier((value, *others))[0]


def per_device(inputs, queries, out_grad, segment_ids, k_weight, v_weight, k_gain):
    tok, depth = inputs.shape
    hd = queries.shape[2]
    heads = queries.shape[1]
    groups = k_weight.shape[1] // hd
    xl, xh, core = lax.axis_index("xl"), lax.axis_index("xh"), lax.axis_index("c")
    xl_array = jnp.full((1,), xl, jnp.int32)
    zero_array = jnp.zeros((1,), jnp.int32)

    def group(g):
        return slice(2 * g * hd, 2 * (g + 1) * hd)

    shard = jnp.concatenate(
        [w[:, g * hd : (g + 1) * hd] for g in range(groups) for w in (k_weight, v_weight)], 1
    )
    half = depth // 2
    some = hop(piece(inputs, jnp.stack([core, 1 - xl]).astype(jnp.int32)), "xl", NX, 1)
    near, gather_rest = gather_half(shard, xl)
    near, seg = lax.optimization_barrier((near, segment_ids))
    own_turned = turned(inputs, after(xl_array, near), half)
    held = {}

    def meanwhile(t, up, down):
        if t == 2:
            up, down, held["turned"] = lax.optimization_barrier((up, down, own_turned))
        return up, down

    weight = gather_rest(near, meanwhile)
    own_turned = held["turned"]
    rest = hop(some, "c", 2, 1)
    par_in = jnp.where(core == 0, join_majors(some, rest), join_majors(rest, some))

    ids = (seg + 1).astype(F32)
    query_seg = ids.reshape(tok // QB, 1, QB)
    key_seg = jnp.zeros((SEG_ROWS, 2 * hd), BF16)
    key_seg = key_seg.at[: tok // (2 * hd)].set(ids.astype(BF16).reshape(-1, 2 * hd))
    q_flat = after(queries, near).reshape(tok, heads * hd)
    do_flat = after(out_grad, near).reshape(tok, heads * hd)

    par_raw = project(par_in, zero_array, weight, groups)
    from_par = [hop(par_raw[0], "xl", NX, 1)]
    from_par.append(hop(after(par_raw[1], from_par[0]), "xl", NX, 1))
    own_raw = project(inputs, after(xl_array, *par_raw), weight, groups)
    par_turned = turned(par_in, after(zero_array, *own_raw), half)
    from_par[0], par_turned = lax.optimization_barrier((from_par[0], par_turned))

    def forward(own_raw, from_par, gain):
        raw = own_raw + from_par
        k_raw = raw[:, :hd]
        k_inv = lax.rsqrt(jnp.mean(k_raw * k_raw, axis=-1, keepdims=True) + 1e-06)
        k_normed = k_raw * k_inv
        own = jnp.concatenate([k_normed * gain, raw[:, hd:]], 1).astype(BF16)
        return join_majors(own, key_seg), k_normed, k_inv

    def attend(own, g):
        one, two = seq_shift(own, 1), seq_shift(own, 2)
        dq, back, mine = attention(
            q_flat[:, group(g)], do_flat[:, group(g)], two, one, own, query_seg
        )
        one, two = seq_shift(back[tok:], -1), seq_shift(back[:tok], -2)
        return dq, mine, one, two

    def backward(k_normed, k_inv, mine, one, two, gain):
        grads = mine + one.astype(F32) + two.astype(F32)
        normed_grad = grads[:, :hd] * gain
        raw_grad = (
            normed_grad - k_normed * jnp.mean(normed_grad * k_normed, axis=-1, keepdims=True)
        ) * k_inv
        return jnp.concatenate([raw_grad, grads[:, hd:]], 1).astype(BF16)

    state = [forward(own_raw[0], from_par[0], k_gain)]
    for g in range(1, groups):
        arrived, gain = after(from_par[g], state[-1][0]), after(k_gain, state[-1][0])
        state.append(forward(own_raw[g], arrived, gain))
    sent = [attend(state[g][0], g) for g in range(groups)]
    dqs = [t[0] for t in sent]
    lows = []
    for g in range(groups):
        mine, one, two = sent[g][1:]
        if lows:
            mine = after(mine, lows[-1])
        gain = after(k_gain, mine)
        lows.append(backward(*state[g][1:], mine, one, two, gain))
    pars = [hop(low, "xl", NX, 1) for low in lows]
    own_grads, par_grads = jnp.concatenate(lows, 1), jnp.concatenate(pars, 1)

    keep = xh == xl
    core_array = jnp.full((1,), core, jnp.int32)
    far = input_term(1 - core_array, weight, own_grads, par_grads)
    received = hop(far, "c", 2, 1)

    def between(t, ahead, behind):
        if t == 4:
            queries_out = jnp.concatenate(dqs, 1).reshape(tok, heads, hd)
            ahead, behind, held["queries"] = lax.optimization_barrier((ahead, behind, queries_out))
        if t == 2:
            own_part, low = input_term(core_array, weight, own_grads, par_grads, received)
            first = jnp.where(keep, low[:, tok:], low[:, :tok])
            held["own"] = own_part
            ahead, behind, held["first"], held["second"] = lax.optimization_barrier(
                (ahead, behind, first, low[:, tok:])
            )
        return ahead, behind

    par_later = after(par_grads, far)
    grad = weight_grad(own_turned, par_turned, own_grads, par_later)
    grad = reduce_half(grad, xl, between)
    cols = [grad[:, i * hd : (i + 1) * hd] for i in range(2 * groups)]
    k_weight_grad = jnp.concatenate(cols[0::2], 1)
    v_weight_grad = jnp.concatenate(cols[1::2], 1)
    query_grad = held["queries"]

    first = lax.ppermute(held["first"], ("xl", "xh"), [(0, 2), (3, 1), (1, 0), (2, 3)])
    second = lax.ppermute(held["second"], ("xl", "xh"), [(1, 2), (2, 1)])
    keep_array = jnp.full((1,), keep, jnp.int32)
    inputs_grad = finish(keep_array, held["own"], first, second)
    return inputs_grad.T, query_grad, k_weight_grad, v_weight_grad


def solution(mesh):
    fine = Mesh(mesh.devices.reshape(NY, NZ, NX, 2, 2), ("y", "z", "xl", "xh", "c"))
    seq, head = ("y", "z", "xl"), ("xh", "c")
    in_specs = (
        P(seq, None),
        P(seq, head, None),
        P(seq, head, None),
        P(seq),
        P(seq, head),
        P(seq, head),
        P(),
    )
    out_specs = (P(seq, head), P(seq, head, None), P(seq, head), P(seq, head))

    return jax.shard_map(
        per_device, mesh=fine, in_specs=in_specs, out_specs=out_specs, check_vma=False
    )
```
